256 devices in a mesh: wide: 64 (over y_hi, z, x), narrow: 4 (over y_lo, core).
Axes of the slice: x: 4, y: 4 (y_hi: 2, y_lo: 2; y = y_hi * 2 + y_lo), z: 8, core: 2. Of those that a mesh axis runs over, the one named last changes fastest.
Arguments:
- image_feats: bfloat16 [12288, 1152], P(('wide', 'narrow')), may hold values from -400 to 400
- proj_weight: bfloat16 [1152, 1152], replicated, may hold values from -0.1875 to 0.1875
- text_embed: bfloat16 [12288, 1152], P(('wide', 'narrow')), may hold values from -400 to 400
- log_scale: float32 [1], replicated, may hold values from 1.6 to 2.4
- logit_bias: float32 [1], replicated, may hold values from -7 to -4
Outputs:
- image_loss: float32 [12288], P(('wide', 'narrow'))
- d_text_unit: float32 [12288, 1152], P(('wide', 'narrow'))
- d_proj: float32 [1152, 1152], P('wide', 'narrow')
The draws below stay inside these ranges and needn't reach their ends.
All inputs are finite; a program needn't handle non-finite values.
Results may differ from the reference program's by a relative error of at most 0.0037.
Values may be sent and summed in bfloat16 or wider, within the bound.
A program may use at most 64 MiB of HBM per device.

```python
import math
import jax
import jax.numpy as jnp
from jax import lax

D = 1152
BATCH = 12288


def scale_factors(key):
    row_key, col_key = jax.random.split(key, 2)
    row_scale = jnp.exp(jax.random.uniform(row_key, (BATCH, 1), jnp.float32) * math.log(10.0))
    col_scale = jnp.exp(jax.random.uniform(col_key, (1, D), jnp.float32) * math.log(10.0))
    return row_scale * col_scale


def draw_image_feats(key, part):
    inner = jax.random.fold_in(key, 11)
    scale_key, noise_key = jax.random.split(inner, 2)
    factors = scale_factors(scale_key)
    noise = jax.random.truncated_normal(noise_key, -4.0, 4.0, (BATCH, D), jnp.float32)
    return (factors * noise).astype(jnp.bfloat16)


def draw_text_embed(key, part):
    inner = jax.random.fold_in(key, 23)
    scale_key, noise_key = jax.random.split(inner, 2)
    factors = scale_factors(scale_key)
    noise = jax.random.truncated_normal(noise_key, -4.0, 4.0, (BATCH, D), jnp.float32)
    return (factors * noise).astype(jnp.bfloat16)


def gaussian(stream_key, dims, spread, most, kind=jnp.bfloat16):
    return jnp.clip(spread * jax.random.normal(stream_key, dims, jnp.float32), -most, most).astype(kind)


def setup_inputs(seed: int = 0) -> dict:
    seeds = jax.random.split(jax.random.key(seed), 6)
    image_feats = draw_image_feats(jax.random.fold_in(seeds[5], 71), 0)
    proj_weight = gaussian(seeds[1], (D, D), D ** -0.5, 0.1875)
    text_embed = draw_text_embed(jax.random.fold_in(seeds[5], 71), 0)
    log_scale = jnp.clip(jax.random.uniform(seeds[3], (1,), jnp.float32, 1.6, 2.4), 1.6, 2.4)
    logit_bias = jnp.clip(jax.random.uniform(seeds[4], (1,), jnp.float32, -7.0, -4.0), -7.0, -4.0)
    return dict(image_feats=image_feats, proj_weight=proj_weight, text_embed=text_embed, log_scale=log_scale, logit_bias=logit_bias)


def unit_rows(values):
    inverse = lax.rsqrt(lax.optimization_barrier(jnp.sum(values * values, axis=1, keepdims=True)) + 1e-06)
    return (values * inverse, inverse)

def reference(image_feats, proj_weight, text_embed, log_scale, logit_bias):
    zproj = jnp.dot(image_feats, proj_weight, preferred_element_type=jnp.float32)
    img_unit, img_inv = unit_rows(zproj)
    img_emb = img_unit.astype(jnp.bfloat16)
    txt_unit, txt_inv = unit_rows(text_embed.astype(jnp.float32))
    txt_emb = txt_unit.astype(jnp.bfloat16)
    logit_scale = jnp.exp(log_scale[0])
    logit_shift = logit_bias[0]
    batch_rows = image_feats.shape[0]
    width = image_feats.shape[1]
    block_rows = math.gcd(batch_rows, 512)
    block_total = batch_rows // block_rows
    caption_idx = jnp.arange(batch_rows, dtype=jnp.int32)

    def one_block(caption_grad, block_id):
        row_start = (block_id * block_rows).astype(jnp.int32)
        rows_img = lax.dynamic_slice_in_dim(img_emb, row_start, block_rows, 0)
        products = jnp.dot(rows_img, txt_emb.T, preferred_element_type=jnp.float32)
        logits = logit_scale * products + logit_shift
        image_idx = row_start + jnp.arange(block_rows, dtype=jnp.int32)
        label_sign = jnp.where(image_idx[:, None] == caption_idx[None, :], 1.0, -1.0).astype(logits.dtype)
        loss_rows = lax.optimization_barrier(jnp.sum(jax.nn.softplus(-label_sign * logits), axis=1))
        grad_tile = (-logit_scale * label_sign * jax.nn.sigmoid(-label_sign * logits)).astype(jnp.bfloat16)
        d_img = jnp.dot(grad_tile, txt_emb, preferred_element_type=jnp.float32)
        caption_grad = caption_grad + jnp.dot(grad_tile.T, rows_img, preferred_element_type=jnp.float32)
        return (caption_grad, (loss_rows, d_img))
    start_grad = jnp.zeros((batch_rows, width), jnp.float32)
    caption_grad, (loss_blocks, d_img_blocks) = lax.scan(one_block, start_grad, jnp.arange(block_total, dtype=jnp.int32))
    image_loss = loss_blocks.reshape(batch_rows)
    d_img = d_img_blocks.reshape(batch_rows, width)
    d_zproj = (img_inv * (d_img - img_unit * lax.optimization_barrier(jnp.sum(img_unit * d_img, axis=1, keepdims=True)))).astype(jnp.bfloat16)
    d_proj = jnp.dot(image_feats.T, d_zproj, preferred_element_type=jnp.float32)
    return (image_loss, caption_grad, d_proj)
```

```python
import functools

import jax
import jax.numpy as jnp
from jax import lax
from jax.experimental import pallas as pl
from jax.experimental.pallas import tpu as pltpu
from jax.sharding import PartitionSpec as P

MESH = pl.DeviceIdType.MESH
F32 = jnp.float32
BF16 = jnp.bfloat16

NX, NY, NZ = 4, 4, 8
STREAM = ("L4", "L3", "S3", "L2", "S2", "L1", "S1", "0")
SLOTS = (
    ("X", "L4"), ("X", "L3"), ("X", "S3"), ("O", "L4"), ("O", "L3"), ("O", "S3"),
    ("X", "L2"), ("X", "S2"), ("O", "L2"), ("O", "S2"),
    ("X", "L1"), ("X", "S1"), ("X", "0"), ("O", "L1"), ("O", "S1"), ("O", "0"),
)
SLOT_ROW = {name: i for i, name in enumerate(SLOTS)}
BATCHES = ((0, 6), (6, 10), (10, 16))
RING = STREAM[:7]
ROW_OF_DQ = {2: 0, 1: 1, 0: 2, 3: 3}


def kernel(
    scale_ref, shift_ref, feats_ref, w_hbm, text_ref,
    loss_out, dtext_out, dproj_out,
    wv, ua, fa, za, ta, g, unit, inv, dimg, lossp, psend, precv, rsend, rrecv,
    dtx, hsend, hrecv, qsend, qrecv, tsend, trecv, fsel, pf, pb, precvb, fin,
    w_sem, a_ring_send, a_ring_recv, a_part_send, a_part_recv,
    b_send, b_recv, ps_sem, pr_sem, rs_sem, rr_sem,
    hs_sem, hr_sem, qs_sem, qr_sem, ts_sem, tr_sem, fs_sem, fr_sem,
):
    rows, width = feats_ref.shape
    chunk = 16
    n_chunk = rows // chunk
    wide = lax.axis_index("wide")
    narrow = lax.axis_index("narrow")
    x = wide % NX
    z = (wide // NX) % NZ
    y = (wide // (NX * NZ)) * 2 + narrow // 2
    core = narrow % 2

    def dev(dx=0, dy=0, dz=0, other=False):
        tx = (x + dx) % NX
        ty = (y + dy) % NY
        tz = (z + dz) % NZ
        tc = (1 - core) if other else core
        return ((ty // 2) * (NX * NZ) + tz * NX + tx, (ty % 2) * 2 + tc)

    def dev_b(dp, dq):
        return dev(dx=dp * (1 - core) + dq * core, dy=dp * core + dq * (1 - core))

    step_z = 1 + core * (NZ - 2)
    along = dev(dz=step_z)
    against = dev(dz=NZ - step_z)
    partner = dev(other=True)

    def rcopy(src, dst, ssem, rsem, target):
        return pltpu.make_async_remote_copy(
            src_ref=src, dst_ref=dst, send_sem=ssem, recv_sem=rsem,
            device_id=target, device_id_type=MESH,
        )

    sends = []

    def send(src, dst, ssem, rsem, target):
        copy = rcopy(src, dst, ssem, rsem, target)
        copy.start()
        sends.append(copy)

    def arrived(dst, ssem, rsem, target):
        rcopy(dst, dst, ssem, rsem, target).wait_recv()

    barrier = pltpu.get_barrier_semaphore()
    peers = [dev_b(dp, dq) for dp in range(4) for dq in range(4) if (dp, dq) != (0, 0)]
    peers += [along, against, partner]
    for peer in peers:
        pl.semaphore_signal(barrier, inc=1, device_id=peer, device_id_type=MESH)
    w_copy = pltpu.make_async_copy(w_hbm, wv, w_sem)
    w_copy.start()

    def part(buf, slot, c):
        return buf.at[pl.ds(SLOT_ROW[slot] * rows + c * chunk, chunk)]

    def a_copy(k, buf, name, c, to_name, target):
        i = STREAM.index(to_name)
        send(
            part(buf, ("O", name), c), part(buf, ("O", to_name), c),
            a_ring_send.at[k, i, c], a_ring_recv.at[k, i, c], target,
        )

    def a_hand(k, buf, name, c):
        i = STREAM.index(name)
        send(
            part(buf, ("O", name), c), part(buf, ("X", name), c),
            a_part_send.at[k, i, c], a_part_recv.at[k, i, c], partner,
        )

    def a_start(k, buf):
        for c in range(n_chunk):
            a_copy(k, buf, "0", c, "L1", along)
            a_copy(k, buf, "0", c, "S1", against)
            a_hand(k, buf, "0", c)

    def a_wait(k, buf, name, c):
        i = STREAM.index(name)
        arrived(part(buf, ("O", name), c), a_ring_send.at[k, i, c], a_ring_recv.at[k, i, c], along)

    def a_step(k, buf, n):
        for c in range(n_chunk):
            a_wait(k, buf, f"L{n}", c)
            if n < 4:
                a_copy(k, buf, f"L{n}", c, f"L{n + 1}", along)
            a_hand(k, buf, f"L{n}", c)
            if n <= 3:
                a_wait(k, buf, f"S{n}", c)
                if n < 3:
                    a_copy(k, buf, f"S{n}", c, f"S{n + 1}", against)
                a_hand(k, buf, f"S{n}", c)

    def a_finish(k, buf):
        for name in STREAM:
            i = STREAM.index(name)
            for c in range(n_chunk):
                arrived(part(buf, ("X", name), c), a_part_send.at[k, i, c], a_part_recv.at[k, i, c], partner)

    def t_slot(dp, dq):
        return ta.at[pl.ds((ROW_OF_DQ[dq % 4] * 4 + dp % 4) * rows, rows)]

    def b_copy(dp, dq, mp, mq):
        to = ((dp - mp) % 4, (dq - mq) % 4)
        send(
            t_slot(dp, dq), t_slot(*to), b_send.at[to[1] * 4 + to[0]], b_recv.at[to[1] * 4 + to[0]],
            dev_b(mp % 4, mq % 4),
        )

    def b_wait(dp, dq):
        i = dq * 4 + dp
        arrived(t_slot(dp, dq), b_send.at[i], b_recv.at[i], partner)

    def b_spread(dp):
        b_copy(dp, 0, 0, 1)
        b_copy(dp, 0, 0, -1)

    text = text_ref[...].astype(F32)
    text_inv = lax.rsqrt(jnp.sum(text * text, axis=1, keepdims=True) + 1e-06)
    own_t = ROW_OF_DQ[0] * 4 * rows
    ta[own_t : own_t + rows] = (text * text_inv).astype(BF16)
    own_u = SLOT_ROW[("O", "0")] * rows
    fa[own_u : own_u + rows] = feats_ref[...]

    pl.semaphore_wait(barrier, len(peers))
    b_copy(0, 0, 1, 0)
    b_copy(0, 0, -1, 0)
    b_spread(0)

    w_copy.wait()
    zproj = jnp.dot(feats_ref[...], wv[...], preferred_element_type=F32)
    img_inv = lax.rsqrt(jnp.sum(zproj * zproj, axis=1, keepdims=True) + 1e-06)
    img_unit = zproj * img_inv
    unit[...] = img_unit
    inv[...] = jnp.broadcast_to(img_inv, inv.shape)
    ua[own_u : own_u + rows] = img_unit.astype(BF16)
    a_start(0, ua)

    b_wait(3, 0)
    b_copy(3, 0, 1, 0)
    b_spread(3)
    b_wait(1, 0)
    b_spread(1)
    a_step(0, ua, 1)
    b_wait(2, 0)
    b_spread(2)
    for dp in (0, 2):
        b_wait(dp, 3)
        b_copy(dp, 3, 0, 1)
    for dp in (3, 1):
        b_wait(dp, 1)
        b_copy(dp, 1, 0, -1)
    a_step(0, ua, 2)
    a_step(0, ua, 3)
    a_start(1, fa)
    a_step(0, ua, 4)
    for dp in (0, 2):
        b_wait(dp, 1)
    for dp in (3, 1):
        b_wait(dp, 3)
    for dp in range(4):
        b_wait(dp, 2)
    a_finish(0, ua)
    a_step(1, fa, 1)

    scale = jnp.exp(jnp.full((1, 128), scale_ref[0], F32))[:, :1]
    shift = shift_ref[0]
    lossp[...] = jnp.zeros_like(lossp)
    half = 8 * rows
    tile = 256

    def pairs(i, carry):
        pair = i // 3
        r0 = pl.multiple_of((i % 3) * tile, tile)
        t0 = pl.multiple_of(pair * half, 16)
        prod = lax.dot_general(
            ua[pl.ds(r0, tile), :], ta[pl.ds(t0, half), :], (((1,), (1,)), ((), ())),
            preferred_element_type=F32,
        )
        total = None
        for j in range(half // 128):
            logit = scale * prod[:, 128 * j : 128 * (j + 1)] + shift
            factor = scale
            if j == 0:
                row = lax.broadcasted_iota(jnp.int32, logit.shape, 0) + (r0 - own_u)
                col = lax.broadcasted_iota(jnp.int32, logit.shape, 1)
                own = jnp.logical_and(row == col, pair == 1)
                logit = jnp.where(own, -logit, logit)
                factor = jnp.where(own, -scale, scale)
            e = jnp.exp(logit)
            g[pair, pl.ds(r0, tile), 128 * j : 128 * (j + 1)] = (factor * (e / (1.0 + e))).astype(BF16)
            term = jnp.log1p(e)
            total = term if total is None else total + term
        lossp[pl.ds(r0, tile), :] += total
        return carry

    lax.fori_loop(0, 6, pairs, 0)
    a_step(1, fa, 2)

    lane = lax.broadcasted_iota(jnp.int32, (rows, 128), 1)

    def slot_rows(slot):
        return pl.ds(SLOT_ROW[slot] * rows, rows)

    def pack(ref, i, value, loss):
        hi = loss.astype(BF16).astype(F32)
        lo = loss - hi
        ref[i, :, :width] = value.astype(BF16)
        ref[i, :, width:] = jnp.where(lane == 0, hi, jnp.where(lane == 1, lo, 0.0)).astype(BF16)

    def unpack(ref, i):
        tail = ref[i, :, width:].astype(F32)
        return ref[i, :, :width].astype(F32), jnp.sum(tail, axis=1, keepdims=True)

    def own_part(slot):
        return dimg[slot_rows(slot), :], jnp.sum(lossp[slot_rows(slot), :], axis=1, keepdims=True)

    def image_batch(b):
        lo, hi = BATCHES[b]
        r = slice(lo * rows, hi * rows)
        acc = jnp.dot(g[0, r, :], ta[:half], preferred_element_type=F32)
        acc += jnp.dot(g[1, r, :], ta[half:], preferred_element_type=F32)
        dimg[r, :] = acc
        for kind, name in SLOTS[lo:hi]:
            if kind == "X":
                i = STREAM.index(name)
                pack(psend, i, *own_part((kind, name)))
                send(psend.at[i], precv.at[i], ps_sem.at[i], pr_sem.at[i], partner)

    def gathered(name):
        i = STREAM.index(name)
        arrived(precv.at[i], ps_sem.at[i], pr_sem.at[i], partner)
        value, loss = own_part(("O", name))
        more, more_loss = unpack(precv, i)
        value, loss = value + more, loss + more_loss
        if name == "0":
            before = ["L1", "S1"]
        elif name in ("L4", "S3"):
            before = []
        else:
            before = [name[0] + str(int(name[1]) + 1)]
        for prev in before:
            j = RING.index(prev)
            arrived(rrecv.at[j], rs_sem.at[j], rr_sem.at[j], along)
            more, more_loss = unpack(rrecv, j)
            value, loss = value + more, loss + more_loss
        return value, loss

    def ring(name):
        i = RING.index(name)
        pack(rsend, i, *gathered(name))
        send(rsend.at[i], rrecv.at[i], rs_sem.at[i], rr_sem.at[i], against if name[0] == "L" else along)

    def caption_half(k):
        dtx[k * half : (k + 1) * half, :] = lax.dot_general(
            g[k], ua[...], (((0,), (0,)), ((), ())), preferred_element_type=F32
        )

    quarter = 4 * rows
    image_batch(0)
    image_batch(1)
    ring("L4")
    ring("S3")
    a_step(1, fa, 3)
    image_batch(2)
    ring("L3")
    caption_half(0)
    hsend[...] = dtx[:quarter].astype(BF16)
    send(hsend.at[: quarter // 2], hrecv.at[0], hs_sem.at[0], hr_sem.at[0], dev_b(0, 1))
    send(hsend.at[quarter // 2 :], hrecv.at[1], hs_sem.at[1], hr_sem.at[1], dev_b(0, 3))
    ring("L2")
    ring("S2")
    a_step(1, fa, 4)
    caption_half(1)

    arrived(hrecv.at[0], hs_sem.at[0], hr_sem.at[0], partner)
    h = quarter // 2
    up, down = quarter, 3 * quarter
    qsend[0, :h] = (dtx[up : up + h] + hrecv[0].astype(F32)).astype(BF16)
    qsend[0, h:] = dtx[up + h : up + quarter].astype(BF16)
    send(qsend.at[0], qrecv.at[0], qs_sem.at[0], qr_sem.at[0], dev_b(0, 1))
    arrived(hrecv.at[1], hs_sem.at[1], hr_sem.at[1], partner)
    qsend[1, :h] = dtx[down : down + h].astype(BF16)
    qsend[1, h:] = (dtx[down + h : down + quarter] + hrecv[1].astype(F32)).astype(BF16)
    send(qsend.at[1], qrecv.at[1], qs_sem.at[1], qr_sem.at[1], dev_b(0, 3))

    ring("L1")
    ring("S1")
    a_finish(1, fa)
    pick_row = lax.broadcasted_iota(jnp.int32, (width, 256), 0)
    pick_col = lax.broadcasted_iota(jnp.int32, (width, 256), 1)
    combo = pick_col >> 5
    inner = pick_col & 31
    wanted = 18 * (32 * (combo >> 2) + 4 * z + (combo & 3)) + inner
    pick = jnp.where(jnp.logical_and(pick_row == wanted, inner < 18), 1.0, 0.0).astype(BF16)
    fsel[...] = jnp.dot(fa[...], pick, preferred_element_type=F32).astype(BF16)

    value, loss = gathered("0")
    loss_out[...] = jnp.broadcast_to(loss, loss_out.shape)
    u = unit[...]
    dz = inv[:, :1] * (value - u * jnp.sum(u * value, axis=1, keepdims=True))
    za[own_u : own_u + rows] = dz.astype(BF16)
    a_start(2, za)

    arrived(qrecv.at[0], qs_sem.at[0], qr_sem.at[0], partner)
    arrived(qrecv.at[1], qs_sem.at[1], qr_sem.at[1], partner)
    base = 2 * quarter

    def mine(dp):
        r = slice(dp * rows, (dp + 1) * rows)
        return dtx[base + dp * rows : base + (dp + 1) * rows] + qrecv[0, r].astype(F32) + qrecv[1, r].astype(F32)

    for dp in (2, 1, 3):
        i = dp - 1
        tsend[i] = mine(dp).astype(BF16)
        send(tsend.at[i], trecv.at[i], ts_sem.at[i], tr_sem.at[i], dev_b(dp, 0))
    a_step(2, za, 1)
    a_step(2, za, 2)
    caption = mine(0)
    for i in range(3):
        arrived(trecv.at[i], ts_sem.at[i], tr_sem.at[i], partner)
        caption = caption + trecv[i].astype(F32)
    dtext_out[...] = caption
    a_step(2, za, 3)
    a_step(2, za, 4)
    a_finish(2, za)

    for yl in range(2):
        c0 = pl.multiple_of(256 * core + 512 * yl, 128)
        out = lax.dot_general(
            fsel[...], za[:, pl.ds(c0, 384)], (((0,), (0,)), ((), ())), preferred_element_type=F32
        )
        out = out.reshape(8, 32, 384)
        pf[yl] = out
        pb[yl] = out.astype(BF16)
    for dx, dy in [(2, 2), (2, 1), (2, 3), (1, 2), (3, 2), (1, 1), (3, 1), (1, 3), (3, 3),
                   (2, 0), (0, 2), (1, 0), (3, 0), (0, 1), (0, 3)]:
        tx, ty = (x + dx) % NX, (y + dy) % NY
        i = ((4 - dy) % 4) * 4 + (4 - dx) % 4
        send(
            pb.at[ty % 2, (ty // 2) * 4 + tx], precvb.at[i], fs_sem.at[i], fr_sem.at[i], dev(dx=dx, dy=dy)
        )
    acc = pf[y % 2, (y // 2) * 4 + x]
    for i in range(1, 16):
        arrived(precvb.at[i], fs_sem.at[i], fr_sem.at[i], partner)
        acc = acc + precvb[i].astype(F32)
    fin[...] = acc
    for n in range(4):
        @pl.when(narrow == n)
        def _():
            dproj_out[...] = fin[:18, 32 * n : 32 * n + 288]

    for copy in sends:
        copy.wait_send()


def local(image_feats, proj_weight, text_embed, log_scale, logit_bias):
    rows, width = image_feats.shape
    vmem = pl.BlockSpec(memory_space=pltpu.VMEM)
    smem = pl.BlockSpec(memory_space=pltpu.SMEM)
    group = 16 * rows
    dma = pltpu.SemaphoreType.DMA
    loss, d_text, d_proj = pl.pallas_call(
        kernel,
        out_shape=(
            jax.ShapeDtypeStruct((rows, 128), F32),
            jax.ShapeDtypeStruct((rows, width), F32),
            jax.ShapeDtypeStruct((width // 64, width // 4), F32),
        ),
        in_specs=[smem, smem, vmem, pl.BlockSpec(memory_space=pl.ANY), vmem],
        out_specs=(vmem, vmem, vmem),
        scratch_shapes=[
            pltpu.VMEM((width, width), BF16),
            pltpu.VMEM((group, width), BF16),
            pltpu.VMEM((group, width), BF16),
            pltpu.VMEM((group, width), BF16),
            pltpu.VMEM((group, width), BF16),
            pltpu.VMEM((2, group, group // 2), BF16),
            pltpu.VMEM((rows, width), F32),
            pltpu.VMEM((rows, 128), F32),
            pltpu.VMEM((group, width), F32),
            pltpu.VMEM((group, 128), F32),
            pltpu.VMEM((8, rows, width + 128), BF16),
            pltpu.VMEM((8, rows, width + 128), BF16),
            pltpu.VMEM((7, rows, width + 128), BF16),
            pltpu.VMEM((7, rows, width + 128), BF16),
            pltpu.VMEM((group, width), F32),
            pltpu.VMEM((4 * rows, width), BF16),
            pltpu.VMEM((2, 2 * rows, width), BF16),
            pltpu.VMEM((2, 4 * rows, width), BF16),
            pltpu.VMEM((2, 4 * rows, width), BF16),
            pltpu.VMEM((3, rows, width), BF16),
            pltpu.VMEM((3, rows, width), BF16),
            pltpu.VMEM((group, 256), BF16),
            pltpu.VMEM((2, 8, 32, 384), F32),
            pltpu.VMEM((2, 8, 32, 384), BF16),
            pltpu.VMEM((16, 32, 384), BF16),
            pltpu.VMEM((32, 384), F32),
            dma,
            dma((3, 8, 3)), dma((3, 8, 3)), dma((3, 8, 3)), dma((3, 8, 3)),
            dma((16,)), dma((16,)),
            dma((8,)), dma((8,)), dma((7,)), dma((7,)),
            dma((2,)), dma((2,)), dma((2,)), dma((2,)), dma((3,)), dma((3,)),
            dma((16,)), dma((16,)),
        ],
        compiler_params=pltpu.CompilerParams(
            collective_id=0, has_side_effects=True, vmem_limit_bytes=60 * 1024 * 1024
        ),
    )(log_scale, logit_bias, image_feats, proj_weight, text_embed)
    return loss[:, 0], d_text, d_proj


def solution(mesh):
    placed = (P(("wide", "narrow"), None), P(), P(("wide", "narrow"), None), P(), P())
    return jax.shard_map(
        local,
        mesh=mesh,
        in_specs=placed,
        out_specs=(P(("wide", "narrow")), P(("wide", "narrow"), None), P("wide", "narrow")),
        check_vma=False,
    )
```

```python
import functools

import jax
import jax.numpy as jnp
from jax import lax
from jax.experimental import pallas as pl
from jax.experimental.pallas import tpu as pltpu
from jax.sharding import PartitionSpec as P

MESH = pl.DeviceIdType.MESH
F32 = jnp.float32
BF16 = jnp.bfloat16

NX, NY, NZ = 4, 4, 8
STREAM = ("L4", "L3", "S3", "L2", "S2", "L1", "S1", "0")
SLOTS = (
    ("X", "L4"), ("X", "L3"), ("X", "S3"), ("O", "L4"), ("O", "L3"), ("O", "S3"),
    ("X", "L2"), ("X", "S2"), ("O", "L2"), ("O", "S2"),
    ("X", "L1"), ("X", "S1"), ("X", "0"), ("O", "L1"), ("O", "S1"), ("O", "0"),
)
SLOT_ROW = {name: i for i, name in enumerate(SLOTS)}
BATCHES = ((0, 6), (6, 10), (10, 16))
RING = STREAM[:7]
ROW_OF_DQ = {2: 0, 1: 1, 0: 2, 3: 3}


def kernel(
    scale_hbm, shift_hbm, feats_hbm, w_hbm, text_hbm,
    loss_hbm, dtext_hbm, dproj_hbm,
    scale_ref, shift_ref, feats_ref, text_ref, wv, ua, za, ta, g, unit, inv, dimg, lossp, psend, precv, rsend, rrecv,
    dtx, hsend, hrecv, qsend, qrecv, tsend, trecv, fsel, fsend, pf, pb, precvb, fin, loss_out, dtext_out, dproj_out,
    in_sem, out_sem, a_send, a_ring_recv, a_part_recv,
    b_send, b_recv, f_send, f_recv, ps_sem, pr_sem, rs_sem, rr_sem,
    hs_sem, hr_sem, qs_sem, qr_sem, ts_sem, tr_sem, fs_sem, fr_sem,
):
    rows, width = feats_ref.shape
    inputs = [
        pltpu.make_async_copy(src, dst, in_sem.at[i])
        for i, (src, dst) in enumerate((
            (text_hbm, text_ref), (feats_hbm, feats_ref), (w_hbm, wv), (scale_hbm, scale_ref), (shift_hbm, shift_ref),
        ))
    ]
    for copy in inputs:
        copy.start()
    chunk = 16
    n_chunk = rows // chunk
    wide = lax.axis_index("wide")
    narrow = lax.axis_index("narrow")
    x = wide % NX
    z = (wide // NX) % NZ
    y = (wide // (NX * NZ)) * 2 + narrow // 2
    core = narrow % 2

    def dev(dx=0, dy=0, dz=0, other=False):
        tx = (x + dx) % NX
        ty = (y + dy) % NY
        tz = (z + dz) % NZ
        tc = (1 - core) if other else core
        return ((ty // 2) * (NX * NZ) + tz * NX + tx, (ty % 2) * 2 + tc)

    def dev_b(dp, dq):
        return dev(dx=dp * (1 - core) + dq * core, dy=dp * core + dq * (1 - core))

    step_z = 1 + core * (NZ - 2)
    along = dev(dz=step_z)
    against = dev(dz=NZ - step_z)
    partner = dev(other=True)

    def rcopy(src, dst, ssem, rsem, target):
        return pltpu.make_async_remote_copy(
            src_ref=src, dst_ref=dst, send_sem=ssem, recv_sem=rsem,
            device_id=target, device_id_type=MESH,
        )

    sends = []

    def send(src, dst, ssem, rsem, target, keep=True):
        copy = rcopy(src, dst, ssem, rsem, target)
        copy.start()
        if keep:
            sends.append(copy)

    def sent(buf, ssem, blocks):
        part_of = buf.at[pl.ds(0, blocks * rows)]
        rcopy(part_of, part_of, ssem, ssem, partner).wait_send()

    def arrived(dst, ssem, rsem, target):
        rcopy(dst, dst, ssem, rsem, target).wait_recv()

    barrier = pltpu.get_barrier_semaphore()
    peers = [dev_b(dp, dq) for dp in range(4) for dq in range(4) if (dp, dq) != (0, 0)]
    hops = [(m, other) for m in range(8) for other in (False, True) if (m, other) != (0, False)]
    peers += [dev(dz=m * step_z, other=other) for m, other in hops]
    for peer in peers:
        pl.semaphore_signal(barrier, inc=1, device_id=peer, device_id_type=MESH)

    def part(buf, slot, c):
        return buf.at[pl.ds(SLOT_ROW[slot] * rows + c * chunk, chunk)]

    def a_copy(k, buf, name, c, to_name, target):
        i = STREAM.index(to_name)
        send(
            part(buf, ("O", name), c), part(buf, ("O", to_name), c),
            a_send.at[k], a_ring_recv.at[k, i, c], target, keep=False,
        )

    def a_hand(k, buf, name, c):
        i = STREAM.index(name)
        send(
            part(buf, ("O", name), c), part(buf, ("X", name), c),
            a_send.at[k], a_part_recv.at[k, i, c], partner, keep=False,
        )

    def a_start(k, buf):
        for c in range(n_chunk):
            a_copy(k, buf, "0", c, "L1", along)
            a_copy(k, buf, "0", c, "S1", against)
            a_hand(k, buf, "0", c)

    def a_wait(k, buf, name, c):
        i = STREAM.index(name)
        arrived(part(buf, ("O", name), c), a_send.at[k], a_ring_recv.at[k, i, c], along)

    def a_step(k, buf, n):
        for c in range(n_chunk):
            a_wait(k, buf, f"L{n}", c)
            if n < 4:
                a_copy(k, buf, f"L{n}", c, f"L{n + 1}", along)
            a_hand(k, buf, f"L{n}", c)
            if n <= 3:
                a_wait(k, buf, f"S{n}", c)
                if n < 3:
                    a_copy(k, buf, f"S{n}", c, f"S{n + 1}", against)
                a_hand(k, buf, f"S{n}", c)

    def a_finish(k, buf, names=STREAM):
        for name in names:
            i = STREAM.index(name)
            for c in range(n_chunk):
                arrived(part(buf, ("X", name), c), a_send.at[k], a_part_recv.at[k, i, c], partner)

    def t_part(dp, dq, c):
        return ta.at[pl.ds((ROW_OF_DQ[dq % 4] * 4 + dp % 4) * rows + c * chunk, chunk)]

    def b_copy(dp, dq, mp, mq, c):
        to = ((dp - mp) % 4, (dq - mq) % 4)
        send(
            t_part(dp, dq, c), t_part(*to, c), b_send, b_recv.at[to[1] * 4 + to[0], c],
            dev_b(mp % 4, mq % 4), keep=False,
        )

    def b_wait(dp, dq, c):
        part_of = t_part(dp, dq, c)
        arrived(part_of, b_send, b_recv.at[dq * 4 + dp, c], partner)

    def b_spread(dp, c):
        b_copy(dp, 0, 0, 1, c)
        b_copy(dp, 0, 0, -1, c)

    def each_chunk(step):
        for c in range(n_chunk):
            step(c)

    def b_start(c):
        b_copy(0, 0, 1, 0, c)
        b_copy(0, 0, -1, 0, c)
        b_spread(0, c)

    def b_first(c):
        b_wait(3, 0, c)
        b_copy(3, 0, 1, 0, c)
        b_spread(3, c)
        b_wait(1, 0, c)
        b_spread(1, c)
        b_wait(0, 1, c)
        b_copy(0, 1, 0, -1, c)

    def b_second(c):
        b_wait(2, 0, c)
        b_spread(2, c)
        b_wait(3, 3, c)
        b_copy(3, 3, 0, 1, c)
        b_wait(1, 1, c)
        b_copy(1, 1, 0, -1, c)

    def b_third(c):
        b_wait(2, 3, c)
        b_copy(2, 3, 0, 1, c)
        b_wait(0, 3, c)
        b_wait(1, 3, c)

    def b_last(c):
        for dp, dq in ((3, 1), (2, 1), (0, 2), (3, 2), (1, 2), (2, 2)):
            b_wait(dp, dq, c)

    inputs[0].wait()
    text = text_ref[...].astype(F32)
    text_inv = lax.rsqrt(jnp.sum(text * text, axis=1, keepdims=True) + 1e-06)
    own_t = ROW_OF_DQ[0] * 4 * rows
    ta[own_t : own_t + rows] = (text * text_inv).astype(BF16)
    own_u = SLOT_ROW[("O", "0")] * rows
    inputs[1].wait()

    pl.semaphore_wait(barrier, len(peers))
    each_chunk(b_start)

    for copy in inputs[2:]:
        copy.wait()
    zproj = jnp.dot(feats_ref[...], wv[...], preferred_element_type=F32)
    img_inv = lax.rsqrt(jnp.sum(zproj * zproj, axis=1, keepdims=True) + 1e-06)
    img_unit = zproj * img_inv
    unit[...] = img_unit
    inv[...] = jnp.broadcast_to(img_inv, inv.shape)
    ua[own_u : own_u + rows] = img_unit.astype(BF16)
    a_start(0, ua)

    pick_row = lax.broadcasted_iota(jnp.int32, (width, 256), 0)
    pick_col = lax.broadcasted_iota(jnp.int32, (width, 256), 1)
    combo = pick_col >> 5
    inner = pick_col & 31
    first = jnp.where(inner < 18, 18 * (32 * (combo >> 2) + (combo & 3)) + inner - pick_row, 4 * width)

    def pick(m):
        tz = (z + m * step_z) % NZ
        chosen = jnp.where(first + 72 * tz == 0, 1.0, 0.0).astype(BF16)
        fsend[m] = jnp.dot(feats_ref[...], chosen, preferred_element_type=F32).astype(BF16)

    def pick_sends():
        r = pl.ds(SLOT_ROW[("O", "0")] * rows, rows)
        fsel[r] = fsend[0]
        for m, other in hops:
            i = SLOT_ROW[("X" if other else "O", f"L{m}" if 1 <= m <= 4 else f"S{8 - m}" if m else "0")]
            send(
                fsend.at[m], fsel.at[pl.ds(i * rows, rows)], f_send, f_recv.at[i],
                dev(dz=m * step_z, other=other), keep=False,
            )

    def pick_wait():
        for i in range(16):
            if i != SLOT_ROW[("O", "0")]:
                arrived(fsel.at[pl.ds(i * rows, rows)], f_send, f_recv.at[i], partner)

    scale = jnp.exp(jnp.full((1, 128), scale_ref[0], F32))[:, :1]
    shift = shift_ref[0]
    half = 8 * rows

    def cell(batch, pair):
        r0, r1 = (rows * b for b in BATCHES[batch])
        prod = lax.dot_general(
            ua[r0:r1, :], ta[pair * half : (pair + 1) * half, :], (((1,), (1,)), ((), ())),
            preferred_element_type=F32,
        )
        total = None
        for j in range(half // 128):
            logit = scale * prod[:, 128 * j : 128 * (j + 1)] + shift
            factor = scale
            if j == 0 and pair == 1 and r1 > own_u:
                row = lax.broadcasted_iota(jnp.int32, logit.shape, 0) + (r0 - own_u)
                own = row == lax.broadcasted_iota(jnp.int32, logit.shape, 1)
                logit = jnp.where(own, -logit, logit)
                factor = jnp.where(own, -scale, scale)
            e = jnp.exp(logit)
            g[pair, r0:r1, 128 * j : 128 * (j + 1)] = (factor * (e / (1.0 + e))).astype(BF16)
            term = jnp.log1p(e)
            total = term if total is None else total + term
        if pair == 1:
            lossp[r0:r1, :] = total
        else:
            lossp[r0:r1, :] += total

    pick(0)
    pick(1)
    each_chunk(b_first)
    a_step(0, ua, 1)
    pick(2)
    pick(3)
    a_step(0, ua, 2)
    each_chunk(b_second)
    pick(4)
    pick(5)
    a_step(0, ua, 3)
    pick(6)
    pick(7)
    each_chunk(b_third)
    a_finish(0, ua, ("0", "L1", "S1"))
    cell(2, 1)
    a_step(0, ua, 4)
    pick_sends()
    a_finish(0, ua, ("L2", "S2"))
    cell(1, 1)
    each_chunk(b_last)
    cell(2, 0)
    cell(1, 0)
    a_finish(0, ua, ("L3", "S3", "L4"))
    cell(0, 1)
    cell(0, 0)

    def slot_rows(slot, c=None):
        if c is None:
            return pl.ds(SLOT_ROW[slot] * rows, rows)
        return pl.ds(SLOT_ROW[slot] * rows + c * chunk, chunk)

    def pack(ref, i, r, value, loss):
        lane = lax.broadcasted_iota(jnp.int32, (value.shape[0], 128), 1)
        hi = loss.astype(BF16).astype(F32)
        lo = loss - hi
        ref[i, r, :width] = value.astype(BF16)
        ref[i, r, width:] = jnp.where(lane == 0, hi, jnp.where(lane == 1, lo, 0.0)).astype(BF16)

    def unpack(ref, i, r):
        tail = ref[i, r, width:].astype(F32)
        return ref[i, r, :width].astype(F32), jnp.sum(tail, axis=1, keepdims=True)

    def own_part(slot, c=None):
        r = slot_rows(slot, c)
        return dimg[r, :], jnp.sum(lossp[r, :], axis=1, keepdims=True)

    def image_batch(b):
        lo, hi = BATCHES[b]
        r = slice(lo * rows, hi * rows)
        acc = jnp.dot(g[0, r, :], ta[:half], preferred_element_type=F32)
        acc += jnp.dot(g[1, r, :], ta[half:], preferred_element_type=F32)
        dimg[r, :] = acc
        for kind, name in SLOTS[lo:hi]:
            if kind == "X":
                i = STREAM.index(name)
                pack(psend, i, slice(0, rows), *own_part((kind, name)))
                send(psend.at[i], precv.at[i], ps_sem.at[i], pr_sem.at[i], partner)

    def handed(name):
        i = STREAM.index(name)
        arrived(precv.at[i], ps_sem.at[i], pr_sem.at[i], partner)

    def gathered(name, c):
        r = slice(c * chunk, (c + 1) * chunk)
        value, loss = own_part(("O", name), c)
        more, more_loss = unpack(precv, STREAM.index(name), r)
        value, loss = value + more, loss + more_loss
        if name == "0":
            before = ["L1", "S1"]
        elif name in ("L4", "S3"):
            before = []
        else:
            before = [name[0] + str(int(name[1]) + 1)]
        for prev in before:
            j = RING.index(prev)
            arrived(rrecv.at[j, r], rs_sem.at[j], rr_sem.at[j, c], along)
            more, more_loss = unpack(rrecv, j, r)
            value, loss = value + more, loss + more_loss
        return value, loss

    def ring(*names):
        for name in names:
            handed(name)
        for c in range(n_chunk):
            r = slice(c * chunk, (c + 1) * chunk)
            for name in names:
                i = RING.index(name)
                pack(rsend, i, r, *gathered(name, c))
                send(
                    rsend.at[i, r], rrecv.at[i, r], rs_sem.at[i], rr_sem.at[i, c],
                    against if name[0] == "L" else along, keep=False,
                )

    def caption_half(k):
        dtx[k * half : (k + 1) * half, :] = lax.dot_general(
            g[k], ua[...], (((0,), (0,)), ((), ())), preferred_element_type=F32
        )

    quarter = 4 * rows
    image_batch(0)
    image_batch(1)
    ring("L4")
    image_batch(2)
    ring("L3", "S3")
    caption_half(0)
    hsend[...] = dtx[:quarter].astype(BF16)
    send(hsend.at[: quarter // 2], hrecv.at[0], hs_sem.at[0], hr_sem.at[0], dev_b(0, 1))
    send(hsend.at[quarter // 2 :], hrecv.at[1], hs_sem.at[1], hr_sem.at[1], dev_b(0, 3))
    ring("L2", "S2")
    caption_half(1)

    arrived(hrecv.at[0], hs_sem.at[0], hr_sem.at[0], partner)
    h = quarter // 2
    up, down = quarter, 3 * quarter
    qsend[0, :h] = (dtx[up : up + h] + hrecv[0].astype(F32)).astype(BF16)
    qsend[0, h:] = dtx[up + h : up + quarter].astype(BF16)
    send(qsend.at[0], qrecv.at[0], qs_sem.at[0], qr_sem.at[0], dev_b(0, 1))
    arrived(hrecv.at[1], hs_sem.at[1], hr_sem.at[1], partner)
    qsend[1, :h] = dtx[down : down + h].astype(BF16)
    qsend[1, h:] = (dtx[down + h : down + quarter] + hrecv[1].astype(F32)).astype(BF16)
    send(qsend.at[1], qrecv.at[1], qs_sem.at[1], qr_sem.at[1], dev_b(0, 3))

    ring("L1", "S1")
    handed("0")
    for c in range(n_chunk):
        r = slice(c * chunk, (c + 1) * chunk)
        value, loss = gathered("0", c)
        loss_out[r, :] = jnp.broadcast_to(loss, (chunk, 128))
        u = unit[r, :]
        dz = inv[r, :1] * (value - u * jnp.sum(u * value, axis=1, keepdims=True))
        za[own_u + c * chunk : own_u + (c + 1) * chunk] = dz.astype(BF16)
        a_copy(1, za, "0", c, "L1", along)
        a_copy(1, za, "0", c, "S1", against)
        a_hand(1, za, "0", c)

    arrived(qrecv.at[0], qs_sem.at[0], qr_sem.at[0], partner)
    arrived(qrecv.at[1], qs_sem.at[1], qr_sem.at[1], partner)
    base = 2 * quarter

    def mine(dp):
        r = slice(dp * rows, (dp + 1) * rows)
        return dtx[base + dp * rows : base + (dp + 1) * rows] + qrecv[0, r].astype(F32) + qrecv[1, r].astype(F32)

    for dp in (2, 1, 3):
        i = dp - 1
        tsend[i] = mine(dp).astype(BF16)
        send(tsend.at[i], trecv.at[i], ts_sem.at[i], tr_sem.at[i], dev_b(dp, 0))
    a_step(1, za, 1)
    a_step(1, za, 2)
    caption = mine(0)
    for i in range(3):
        arrived(trecv.at[i], ts_sem.at[i], tr_sem.at[i], partner)
        caption = caption + trecv[i].astype(F32)
    dtext_out[...] = caption
    outputs = [
        pltpu.make_async_copy(src, dst, out_sem.at[i])
        for i, (src, dst) in enumerate(((loss_out, loss_hbm), (dtext_out, dtext_hbm), (dproj_out, dproj_hbm)))
    ]
    outputs[0].start()
    outputs[1].start()
    a_step(1, za, 3)
    a_step(1, za, 4)
    a_finish(1, za)

    pick_wait()
    for yl in range(2):
        c0 = pl.multiple_of(256 * core + 512 * yl, 128)
        out = lax.dot_general(
            fsel[...], za[:, pl.ds(c0, 384)], (((0,), (0,)), ((), ())), preferred_element_type=F32
        )
        out = out.reshape(8, 32, 384)
        pf[yl] = out
        pb[yl] = out.astype(BF16)
    for dx, dy in [(2, 2), (2, 1), (2, 3), (1, 2), (3, 2), (1, 1), (3, 1), (1, 3), (3, 3),
                   (2, 0), (0, 2), (1, 0), (3, 0), (0, 1), (0, 3)]:
        tx, ty = (x + dx) % NX, (y + dy) % NY
        i = ((4 - dy) % 4) * 4 + (4 - dx) % 4
        send(
            pb.at[ty % 2, (ty // 2) * 4 + tx], precvb.at[i], fs_sem.at[i], fr_sem.at[i], dev(dx=dx, dy=dy)
        )
    acc = pf[y % 2, (y // 2) * 4 + x]
    for i in range(1, 16):
        arrived(precvb.at[i], fs_sem.at[i], fr_sem.at[i], partner)
        acc = acc + precvb[i].astype(F32)
    fin[...] = acc
    for n in range(4):
        @pl.when(narrow == n)
        def _():
            dproj_out[...] = fin[:18, 32 * n : 32 * n + 288]

    outputs[2].start()
    for copy in sends:
        copy.wait_send()
    for i in range(7):
        rcopy(rsend.at[i], rsend.at[i], rs_sem.at[i], rs_sem.at[i], partner).wait_send()
    for k, buf in enumerate((ua, za)):
        sent(buf, a_send.at[k], 15)
    sent(ta, b_send, 15)
    sent(fsel, f_send, 15)
    for copy in outputs:
        copy.wait()


def results(loss_ref, dtext_ref, dproj_ref, loss_out, dtext_out, dproj_out):
    loss_out[...] = jnp.transpose(loss_ref[...])[:1, :]
    dtext_out[...] = dtext_ref[...]
    dproj_out[...] = dproj_ref[...]


def local(image_feats, proj_weight, text_embed, log_scale, logit_bias):
    rows, width = image_feats.shape
    vmem = pl.BlockSpec(memory_space=pltpu.VMEM)
    anywhere = pl.BlockSpec(memory_space=pl.ANY)
    group = 16 * rows
    dma = pltpu.SemaphoreType.DMA
    loss, d_text, d_proj = pl.pallas_call(
        kernel,
        out_shape=(
            jax.ShapeDtypeStruct((rows, 128), F32),
            jax.ShapeDtypeStruct((rows, width), F32),
            jax.ShapeDtypeStruct((width // 64, width // 4), F32),
        ),
        in_specs=[anywhere] * 5,
        out_specs=(anywhere, anywhere, anywhere),
        scratch_shapes=[
            pltpu.SMEM((1,), F32),
            pltpu.SMEM((1,), F32),
            pltpu.VMEM((rows, width), BF16),
            pltpu.VMEM((rows, width), BF16),
            pltpu.VMEM((width, width), BF16),
            pltpu.VMEM((group, width), BF16),
            pltpu.VMEM((group, width), BF16),
            pltpu.VMEM((group, width), BF16),
            pltpu.VMEM((2, group, group // 2), BF16),
            pltpu.VMEM((rows, width), F32),
            pltpu.VMEM((rows, 128), F32),
            pltpu.VMEM((group, width), F32),
            pltpu.VMEM((group, 128), F32),
            pltpu.VMEM((8, rows, width + 128), BF16),
            pltpu.VMEM((8, rows, width + 128), BF16),
            pltpu.VMEM((7, rows, width + 128), BF16),
            pltpu.VMEM((7, rows, width + 128), BF16),
            pltpu.VMEM((group, width), F32),
            pltpu.VMEM((4 * rows, width), BF16),
            pltpu.VMEM((2, 2 * rows, width), BF16),
            pltpu.VMEM((2, 4 * rows, width), BF16),
            pltpu.VMEM((2, 4 * rows, width), BF16),
            pltpu.VMEM((3, rows, width), BF16),
            pltpu.VMEM((3, rows, width), BF16),
            pltpu.VMEM((group, 256), BF16),
            pltpu.VMEM((8, rows, 256), BF16),
            pltpu.VMEM((2, 8, 32, 384), F32),
            pltpu.VMEM((2, 8, 32, 384), BF16),
            pltpu.VMEM((16, 32, 384), BF16),
            pltpu.VMEM((32, 384), F32),
            pltpu.VMEM((rows, 128), F32),
            pltpu.VMEM((rows, width), F32),
            pltpu.VMEM((width // 64, width // 4), F32),
            dma((5,)), dma((3,)), dma((2,)), dma((2, 8, 3)), dma((2, 8, 3)),
            dma, dma((16, 3)), dma, dma((16,)),
            dma((8,)), dma((8,)), dma((7,)), dma((7, 3)),
            dma((2,)), dma((2,)), dma((2,)), dma((2,)), dma((3,)), dma((3,)),
            dma((16,)), dma((16,)),
        ],
        compiler_params=pltpu.CompilerParams(
            collective_id=0, has_side_effects=True, vmem_limit_bytes=60 * 1024 * 1024
        ),
    )(log_scale, logit_bias, image_feats, proj_weight, text_embed)
    loss, d_text, d_proj = pl.pallas_call(
        results,
        out_shape=(
            jax.ShapeDtypeStruct((1, rows), F32),
            jax.ShapeDtypeStruct(d_text.shape, F32),
            jax.ShapeDtypeStruct(d_proj.shape, F32),
        ),
        in_specs=[vmem, vmem, vmem],
        out_specs=(vmem, vmem, vmem),
    )(loss, d_text, d_proj)
    return loss.reshape(rows), d_text, d_proj


def solution(mesh):
    placed = (P(("wide", "narrow"), None), P(), P(("wide", "narrow"), None), P(), P())
    return jax.shard_map(
        local,
        mesh=mesh,
        in_specs=placed,
        out_specs=(P(("wide", "narrow")), P(("wide", "narrow"), None), P("wide", "narrow")),
        check_vma=False,
    )
```

```python
import functools

import jax
import jax.numpy as jnp
from jax import lax
from jax.experimental import pallas as pl
from jax.experimental.pallas import tpu as pltpu
from jax.sharding import PartitionSpec as P

MESH = pl.DeviceIdType.MESH
F32 = jnp.float32
BF16 = jnp.bfloat16

NX, NY, NZ = 4, 4, 8
STREAM = ("L4", "L3", "S3", "L2", "S2", "L1", "S1", "0")
SLOTS = (
    ("X", "L4"), ("X", "L3"), ("X", "S3"), ("O", "L4"), ("O", "L3"), ("O", "S3"),
    ("X", "L2"), ("X", "S2"), ("O", "L2"), ("O", "S2"),
    ("X", "L1"), ("X", "S1"), ("X", "0"), ("O", "L1"), ("O", "S1"), ("O", "0"),
)
SLOT_ROW = {name: i for i, name in enumerate(SLOTS)}
BATCHES = ((0, 6), (6, 10), (10, 16))
RING = STREAM[:7]
ROW_OF_DQ = {2: 0, 1: 1, 0: 2, 3: 3}


def kernel(
    scale_hbm, shift_hbm, feats_hbm, w_hbm, text_hbm,
    loss_hbm, dtext_hbm, dproj_hbm,
    scale_ref, shift_ref, feats_ref, text_ref, wv, ta, ub, fb, g, loss_acc, loss_send, loss_recv,
    d_text, psend, precv, rsend, rrecv, dzb, qf, qb, pq, qs, qo, qr, ps, pr, fz, zf, zs, zr, fin,
    loss_out, dtext_out, dproj_out,
    in_sem, out_sem, a_send, a_ring_recv, a_part_recv, b_send, b_recv, f_send, f_recv,
    l_send, l_recv, ps_sem, pr_sem, rs_sem, rr_sem, pq_send, pq_recv,
    qs_sem, qr_sem, ts_sem, tr_sem, zs_sem, zr_sem,
):
    rows, width = feats_ref.shape
    inputs = [
        pltpu.make_async_copy(src, dst, in_sem.at[i])
        for i, (src, dst) in enumerate((
            (text_hbm, text_ref), (feats_hbm, feats_ref), (w_hbm, wv), (scale_hbm, scale_ref), (shift_hbm, shift_ref),
        ))
    ]
    for copy in inputs:
        copy.start()
    chunk = 16
    n_chunk = rows // chunk
    wide = lax.axis_index("wide")
    narrow = lax.axis_index("narrow")
    x = wide % NX
    z = (wide // NX) % NZ
    y = (wide // (NX * NZ)) * 2 + narrow // 2
    core = narrow % 2

    def dev(dx=0, dy=0, dz=0, other=False):
        tx = (x + dx) % NX
        ty = (y + dy) % NY
        tz = (z + dz) % NZ
        tc = (1 - core) if other else core
        return ((ty // 2) * (NX * NZ) + tz * NX + tx, (ty % 2) * 2 + tc)

    def dev_b(dp, dq):
        return dev(dx=dp * (1 - core) + dq * core, dy=dp * core + dq * (1 - core))

    step_z = 1 + core * (NZ - 2)
    along = dev(dz=step_z)
    against = dev(dz=NZ - step_z)
    partner = dev(other=True)

    def rcopy(src, dst, ssem, rsem, target):
        return pltpu.make_async_remote_copy(
            src_ref=src, dst_ref=dst, send_sem=ssem, recv_sem=rsem,
            device_id=target, device_id_type=MESH,
        )

    sends = []

    def send(src, dst, ssem, rsem, target, keep=True):
        copy = rcopy(src, dst, ssem, rsem, target)
        copy.start()
        if keep:
            sends.append(copy)

    def sent(part_of, ssem):
        rcopy(part_of, part_of, ssem, ssem, partner).wait_send()

    def arrived(dst, rsem):
        rcopy(dst, dst, rsem, rsem, partner).wait_recv()

    barrier = pltpu.get_barrier_semaphore()
    peers = [dev_b(dp, dq) for dp in range(4) for dq in range(4) if (dp, dq) != (0, 0)]
    peers += [dev(dz=dz) for dz in range(1, 8)] + [partner]
    for peer in peers:
        pl.semaphore_signal(barrier, inc=1, device_id=peer, device_id_type=MESH)

    def a_part(slot, c):
        return ta.at[pl.ds(SLOT_ROW[slot] * rows + c * chunk, chunk)]

    def a_copy(name, c, to_name, target):
        i = STREAM.index(to_name)
        send(a_part(("O", name), c), a_part(("O", to_name), c), a_send, a_ring_recv.at[i, c], target, keep=False)

    def a_hand(name, c):
        i = STREAM.index(name)
        send(a_part(("O", name), c), a_part(("X", name), c), a_send, a_part_recv.at[i, c], partner, keep=False)

    def a_start():
        for c in range(n_chunk):
            a_copy("0", c, "L1", along)
            a_copy("0", c, "S1", against)
            a_hand("0", c)

    def a_wait(name, c):
        arrived(a_part(("O", name), c), a_ring_recv.at[STREAM.index(name), c])

    def a_step(n):
        for c in range(n_chunk):
            a_wait(f"L{n}", c)
            if n < 4:
                a_copy(f"L{n}", c, f"L{n + 1}", along)
            a_hand(f"L{n}", c)
            if n <= 3:
                a_wait(f"S{n}", c)
                if n < 3:
                    a_copy(f"S{n}", c, f"S{n + 1}", against)
                a_hand(f"S{n}", c)

    def a_finish(*names):
        for name in names:
            for c in range(n_chunk):
                arrived(a_part(("X", name), c), a_part_recv.at[STREAM.index(name), c])

    class Plane:
        def __init__(self, buf, ssem, rsem, size):
            self.buf, self.ssem, self.rsem, self.size = buf, ssem, rsem, size

        def part(self, dp, dq, c):
            return self.buf.at[pl.ds((ROW_OF_DQ[dq % 4] * 4 + dp % 4) * rows + c * self.size, self.size)]

        def copy(self, dp, dq, mp, mq, c):
            to = ((dp - mp) % 4, (dq - mq) % 4)
            send(
                self.part(dp, dq, c), self.part(*to, c), self.ssem, self.rsem.at[to[1] * 4 + to[0], c],
                dev_b(mp % 4, mq % 4), keep=False,
            )

        def wait(self, dp, dq, c):
            arrived(self.part(dp, dq, c), self.rsem.at[dq * 4 + dp, c])

        def spread(self, dp, c):
            self.copy(dp, 0, 0, 1, c)
            self.copy(dp, 0, 0, -1, c)

        def start(self, c):
            self.copy(0, 0, 1, 0, c)
            self.copy(0, 0, -1, 0, c)
            self.spread(0, c)

        def first(self, c):
            self.wait(3, 0, c)
            self.copy(3, 0, 1, 0, c)
            self.spread(3, c)
            self.wait(1, 0, c)
            self.spread(1, c)
            self.wait(0, 1, c)
            self.copy(0, 1, 0, -1, c)

        def second(self, c):
            self.wait(2, 0, c)
            self.spread(2, c)
            self.wait(3, 3, c)
            self.copy(3, 3, 0, 1, c)
            self.wait(1, 1, c)
            self.copy(1, 1, 0, -1, c)

        def third(self, c):
            self.wait(2, 3, c)
            self.copy(2, 3, 0, 1, c)
            self.wait(0, 3, c)
            self.wait(1, 3, c)

        def last(self, c):
            for dp, dq in ((3, 1), (2, 1), (0, 2), (3, 2), (1, 2), (2, 2)):
                self.wait(dp, dq, c)

        def run(self, step):
            for c in range(rows // self.size):
                step(c)

    images = Plane(ub, b_send, b_recv, chunk)
    feats = Plane(fb, f_send, f_recv, rows)

    inputs[0].wait()
    text = text_ref[...].astype(F32)
    text_inv = lax.rsqrt(jnp.sum(text * text, axis=1, keepdims=True) + 1e-06)
    own_a = SLOT_ROW[("O", "0")] * rows
    own_b = ROW_OF_DQ[0] * 4 * rows
    ta[own_a : own_a + rows] = (text * text_inv).astype(BF16)
    inputs[1].wait()
    zs[...] = jnp.zeros_like(zs)
    loss_send[...] = jnp.zeros_like(loss_send)

    pl.semaphore_wait(barrier, len(peers))
    a_start()

    for copy in inputs[2:]:
        copy.wait()
    zproj = jnp.dot(feats_ref[...], wv[...], preferred_element_type=F32)
    img_inv = lax.rsqrt(jnp.sum(zproj * zproj, axis=1, keepdims=True) + 1e-06)
    ub[own_b : own_b + rows] = (zproj * img_inv).astype(BF16)
    images.run(images.start)

    col = lax.broadcasted_iota(jnp.int32, (8, width), 1)
    combo = (col * 911) >> 17
    rest = col - 144 * combo
    layer = (rest * 3641) >> 16
    source = 18 * (32 * (combo >> 2) + 4 * layer + (combo & 3)) + rest - 18 * layer
    order = jnp.where(lax.broadcasted_iota(jnp.int32, (width, width), 0) == source[:1], 1.0, 0.0).astype(BF16)
    fb[own_b : own_b + rows, :width] = jnp.dot(feats_ref[...], order, preferred_element_type=F32).astype(BF16)
    lane = lax.broadcasted_iota(jnp.int32, (rows, 128), 1)
    inv_hi = img_inv.astype(BF16).astype(F32)
    fb[own_b : own_b + rows, width:] = jnp.where(
        lane == 0, inv_hi, jnp.where(lane == 1, img_inv - inv_hi, 0.0)
    ).astype(BF16)

    scale = jnp.exp(jnp.full((1, 128), scale_ref[0], F32))[:, :1]
    shift = shift_ref[0]
    half = 8 * rows

    def cell(batch, pair):
        r0, r1 = (rows * b for b in BATCHES[batch])
        prod = lax.dot_general(
            ta[r0:r1, :], ub[pair * half : (pair + 1) * half, :], (((1,), (1,)), ((), ())),
            preferred_element_type=F32,
        )
        for j in range(half // 128):
            lanes = slice(128 * j, 128 * (j + 1))
            logit = scale * prod[:, lanes] + shift
            factor = scale
            if j == 0 and pair == 1 and r1 > own_a:
                row = lax.broadcasted_iota(jnp.int32, logit.shape, 0) + (r0 - own_a)
                own = row == lax.broadcasted_iota(jnp.int32, logit.shape, 1)
                logit = jnp.where(own, -logit, logit)
                factor = jnp.where(own, -scale, scale)
            e = jnp.exp(logit)
            g[pair, r0:r1, lanes] = (factor * (e / (1.0 + e))).astype(BF16)
            total = jnp.sum(jnp.log1p(e).reshape((r1 - r0) // 8, 8, 128), axis=0)
            if batch == 2:
                loss_acc[pair, :, lanes] = total
            else:
                loss_acc[pair, :, lanes] += total

    a_step(1)
    images.run(images.first)
    a_step(2)
    images.run(images.second)
    a_step(3)
    images.run(images.third)
    a_finish("0", "L1", "S1")
    cell(2, 1)
    a_step(4)
    feats.run(feats.start)
    a_finish("L2", "S2")
    cell(1, 1)
    images.run(images.last)
    cell(2, 0)
    cell(1, 0)
    feats.run(feats.first)
    a_finish("L3", "S3", "L4")
    cell(0, 1)
    cell(0, 0)

    def image_half(pair):
        r = slice(pair * half, (pair + 1) * half)
        d = lax.dot_general(g[pair], ta[...], (((0,), (0,)), ((), ())), preferred_element_type=F32)
        u = ub[r, :].astype(F32)
        factor = jnp.sum(fb[r, width:].astype(F32), axis=1, keepdims=True)
        dzb[r, :] = (factor * (d - u * jnp.sum(u * d, axis=1, keepdims=True))).astype(BF16)

    for pair in range(2):
        summed = jnp.sum(loss_acc[pair], axis=0, keepdims=True)
        for k in range(8):
            loss_send[8 * pair + k, :1, :rows] = summed[:, k * rows : (k + 1) * rows]
    for dq in range(4):
        for dp in range(4):
            if (dp, dq) != (0, 0):
                i = ((4 - dq) % 4) * 4 + (4 - dp) % 4
                k = ROW_OF_DQ[dq] * 4 + dp
                send(loss_send.at[k], loss_recv.at[i], l_send, l_recv.at[i], dev_b(dp, dq), keep=False)

    feats.run(feats.second)
    feats.run(feats.third)
    feats.run(feats.last)
    image_half(1)
    image_half(0)

    block = 384
    for b in range(width // block):
        r = slice(b * block, (b + 1) * block)
        out = lax.dot_general(fb[:, r], dzb[...], (((0,), (0,)), ((), ())), preferred_element_type=F32)
        qf[r, :] = out
        qb[r, :] = out.astype(BF16)
        for yl in range(2):
            lanes = pl.ds(pl.multiple_of(256 * (1 - core) + 512 * yl, 128), 384)
            send(qb.at[r, lanes], pq.at[yl, r], pq_send.at[b, yl], pq_recv.at[b, yl], partner)

    def slot_rows(slot, c=None):
        if c is None:
            return pl.ds(SLOT_ROW[slot] * rows, rows)
        return pl.ds(SLOT_ROW[slot] * rows + c * chunk, chunk)

    def text_batch(b):
        lo, hi = BATCHES[b]
        r = slice(lo * rows, hi * rows)
        acc = jnp.dot(g[0, r, :], ub[:half], preferred_element_type=F32)
        acc += jnp.dot(g[1, r, :], ub[half:], preferred_element_type=F32)
        d_text[r, :] = acc
        for kind, name in SLOTS[lo:hi]:
            if kind == "X":
                i = STREAM.index(name)
                psend[i] = d_text[slot_rows((kind, name)), :].astype(BF16)
                send(psend.at[i], precv.at[i], ps_sem.at[i], pr_sem.at[i], partner)

    def handed(name):
        i = STREAM.index(name)
        arrived(precv.at[i], pr_sem.at[i])

    def gathered(name, c):
        r = slice(c * chunk, (c + 1) * chunk)
        value = d_text[slot_rows(("O", name), c), :] + precv[STREAM.index(name), r].astype(F32)
        if name == "0":
            before = ["L1", "S1"]
        elif name in ("L4", "S3"):
            before = []
        else:
            before = [name[0] + str(int(name[1]) + 1)]
        for prev in before:
            j = RING.index(prev)
            arrived(rrecv.at[j, r], rr_sem.at[j, c])
            value = value + rrecv[j, r].astype(F32)
        return value

    def ring(*names):
        for name in names:
            handed(name)
        for c in range(n_chunk):
            r = slice(c * chunk, (c + 1) * chunk)
            for name in names:
                i = RING.index(name)
                rsend[i, r] = gathered(name, c).astype(BF16)
                send(
                    rsend.at[i, r], rrecv.at[i, r], rs_sem.at[i], rr_sem.at[i, c],
                    against if name[0] == "L" else along, keep=False,
                )

    def unit(dp, dq):
        px = (x + dp * (1 - core) + dq * core) % NX
        py = (y + dp * core + dq * (1 - core)) % NY
        r = pl.ds(pl.multiple_of(144 * ((py // 2) * NX + px), 16), 144)
        lanes = pl.ds(pl.multiple_of(256 * core + 512 * (py % 2), 128), 384)
        return qf[r, lanes] + pq[py % 2, r, :].astype(F32)

    text_batch(0)
    for b in range(width // block):
        for yl in range(2):
            arrived(pq.at[yl, pl.ds(b * block, block)], pq_recv.at[b, yl])
    for dq in (2, 1, 3):
        for dp in range(4):
            qs[dq - 1, dp] = unit(dp, dq).astype(BF16)
        send(qs.at[dq - 1], qr.at[dq - 1], qs_sem.at[dq - 1], qr_sem.at[dq - 1], dev_b(0, dq))
    for dp in range(4):
        qo[dp] = unit(dp, 0)
    text_batch(1)
    ring("L4")
    text_batch(2)
    ring("L3", "S3")
    for i in (0, 2, 1):
        arrived(qr.at[i], qr_sem.at[i])

    def mine(dp):
        return qo[dp] + (qr[0, dp].astype(F32) + qr[1, dp].astype(F32) + qr[2, dp].astype(F32))

    for dp in (2, 1, 3):
        ps[dp - 1] = mine(dp).astype(BF16)
        send(ps.at[dp - 1], pr.at[dp - 1], ts_sem.at[dp - 1], tr_sem.at[dp - 1], dev_b(dp, 0))
    own = mine(0)
    ring("L2", "S2")
    for i in (0, 2, 1):
        arrived(pr.at[i], tr_sem.at[i])
        own = own + pr[i].astype(F32)
    fz[...] = own
    for tz in range(NZ):
        piece = fz[18 * tz : 18 * tz + 18, :]
        zf[tz, :18] = piece
        zs[tz, :18] = piece.astype(BF16)
    for dz in (4, 3, 5, 2, 6, 1, 7):
        send(zs.at[(z + dz) % NZ], zr.at[NZ - dz], zs_sem.at[dz], zr_sem.at[NZ - dz], dev(dz=dz))
    ring("L1", "S1")

    handed("0")
    for c in range(n_chunk):
        dtext_out[c * chunk : (c + 1) * chunk] = gathered("0", c)
    loss = loss_send[ROW_OF_DQ[0] * 4]
    for i in range(1, 16):
        arrived(loss_recv.at[i], l_recv.at[i])
        loss = loss + loss_recv[i]
    loss_out[...] = loss
    outputs = [
        pltpu.make_async_copy(src, dst, out_sem.at[i])
        for i, (src, dst) in enumerate(((loss_out, loss_hbm), (dtext_out, dtext_hbm), (dproj_out, dproj_hbm)))
    ]
    outputs[0].start()
    outputs[1].start()
    acc = zf[z, :18]
    for dz in range(1, 8):
        arrived(zr.at[dz], zr_sem.at[dz])
        acc = acc + zr[dz, :18].astype(F32)
    fin[:18] = acc
    for n in range(4):
        @pl.when(narrow == n)
        def _():
            dproj_out[...] = fin[:18, 32 * n : 32 * n + 288]

    outputs[2].start()
    for copy in sends:
        copy.wait_send()
    for i in range(7):
        sent(rsend.at[i], rs_sem.at[i])
    sent(ta.at[pl.ds(0, 15 * rows)], a_send)
    sent(ub.at[pl.ds(0, 15 * rows)], b_send)
    sent(fb.at[pl.ds(0, 15 * rows)], f_send)
    sent(loss_send.at[pl.ds(0, 15)], l_send)
    for copy in outputs:
        copy.wait()


def results(loss_ref, dtext_ref, dproj_ref, loss_out, dtext_out, dproj_out):
    loss_out[...] = loss_ref[:1, : loss_out.shape[1]]
    dtext_out[...] = dtext_ref[...]
    dproj_out[...] = dproj_ref[...]


def local(image_feats, proj_weight, text_embed, log_scale, logit_bias):
    rows, width = image_feats.shape
    vmem = pl.BlockSpec(memory_space=pltpu.VMEM)
    anywhere = pl.BlockSpec(memory_space=pl.ANY)
    group = 16 * rows
    dma = pltpu.SemaphoreType.DMA
    loss, d_text, d_proj = pl.pallas_call(
        kernel,
        out_shape=(
            jax.ShapeDtypeStruct((8, 128), F32),
            jax.ShapeDtypeStruct((rows, width), F32),
            jax.ShapeDtypeStruct((width // 64, width // 4), F32),
        ),
        in_specs=[anywhere] * 5,
        out_specs=(anywhere, anywhere, anywhere),
        scratch_shapes=[
            pltpu.SMEM((1,), F32),
            pltpu.SMEM((1,), F32),
            pltpu.VMEM((rows, width), BF16),
            pltpu.VMEM((rows, width), BF16),
            pltpu.VMEM((width, width), BF16),
            pltpu.VMEM((group, width), BF16),
            pltpu.VMEM((group, width), BF16),
            pltpu.VMEM((group, width + 128), BF16),
            pltpu.VMEM((2, group, group // 2), BF16),
            pltpu.VMEM((2, 8, group // 2), F32),
            pltpu.VMEM((16, 8, 128), F32),
            pltpu.VMEM((16, 8, 128), F32),
            pltpu.VMEM((group, width), F32),
            pltpu.VMEM((8, rows, width), BF16),
            pltpu.VMEM((8, rows, width), BF16),
            pltpu.VMEM((7, rows, width), BF16),
            pltpu.VMEM((7, rows, width), BF16),
            pltpu.VMEM((group, width), BF16),
            pltpu.VMEM((width, width), F32),
            pltpu.VMEM((width, width), BF16),
            pltpu.VMEM((2, width, 384), BF16),
            pltpu.VMEM((3, 4, 144, 384), BF16),
            pltpu.VMEM((4, 144, 384), F32),
            pltpu.VMEM((3, 4, 144, 384), BF16),
            pltpu.VMEM((3, 144, 384), BF16),
            pltpu.VMEM((3, 144, 384), BF16),
            pltpu.VMEM((144, 384), F32),
            pltpu.VMEM((8, 24, 384), F32),
            pltpu.VMEM((8, 32, 384), BF16),
            pltpu.VMEM((8, 32, 384), BF16),
            pltpu.VMEM((24, 384), F32),
            pltpu.VMEM((8, 128), F32),
            pltpu.VMEM((rows, width), F32),
            pltpu.VMEM((width // 64, width // 4), F32),
            dma((5,)), dma((3,)), dma, dma((8, 3)), dma((8, 3)),
            dma, dma((16, 3)), dma, dma((16, 1)),
            dma, dma((16,)), dma((8,)), dma((8,)), dma((7,)), dma((7, 3)),
            dma((3, 2)), dma((3, 2)),
            dma((3,)), dma((3,)), dma((3,)), dma((3,)), dma((8,)), dma((8,)),
        ],
        compiler_params=pltpu.CompilerParams(
            collective_id=0, has_side_effects=True, vmem_limit_bytes=60 * 1024 * 1024
        ),
    )(log_scale, logit_bias, image_feats, proj_weight, text_embed)
    loss, d_text, d_proj = pl.pallas_call(
        results,
        out_shape=(
            jax.ShapeDtypeStruct((1, rows), F32),
            jax.ShapeDtypeStruct(d_text.shape, F32),
            jax.ShapeDtypeStruct(d_proj.shape, F32),
        ),
        in_specs=[vmem, vmem, vmem],
        out_specs=(vmem, vmem, vmem),
    )(loss, d_text, d_proj)
    return loss.reshape(rows), d_text, d_proj


def solution(mesh):
    placed = (P(("wide", "narrow"), None), P(), P(("wide", "narrow"), None), P(), P())
    return jax.shard_map(
        local,
        mesh=mesh,
        in_specs=placed,
        out_specs=(P(("wide", "narrow")), P(("wide", "narrow"), None), P("wide", "narrow")),
        check_vma=False,
    )
```

```python
import functools

import jax
import jax.numpy as jnp
from jax import lax
from jax.experimental import pallas as pl
from jax.experimental.pallas import tpu as pltpu
from jax.sharding import PartitionSpec as P

MESH = pl.DeviceIdType.MESH
F32 = jnp.float32
BF16 = jnp.bfloat16

NX, NY, NZ = 4, 4, 8
STREAM = ("L4", "L3", "S3", "L2", "S2", "L1", "S1", "0")
SLOTS = (
    ("X", "L4"), ("X", "L3"), ("X", "S3"), ("O", "L4"), ("O", "L3"), ("O", "S3"),
    ("X", "L2"), ("X", "S2"), ("O", "L2"), ("O", "S2"),
    ("X", "L1"), ("X", "S1"), ("X", "0"), ("O", "L1"), ("O", "S1"), ("O", "0"),
)
SLOT_ROW = {name: i for i, name in enumerate(SLOTS)}
BATCHES = ((0, 6), (6, 10), (10, 16))
RING = STREAM[:7]
ROW_OF_DQ = {2: 0, 1: 1, 0: 2, 3: 3}


def kernel(
    scale_hbm, shift_hbm, feats_hbm, w_hbm, text_hbm,
    loss_hbm, dtext_hbm, dproj_hbm,
    scale_ref, shift_ref, feats_ref, text_ref, wv, order, wp, ta, ub, fb, inv, g, loss_acc, loss_send, loss_recv,
    d_text, psend, precv, rsend, rrecv, dzb, qf, qb, pq, qs, qo, qr, ps, pr, fz, zf, zs, zr, fin,
    loss_out, dtext_out, dproj_out,
    in_sem, out_sem, a_send, a_ring_recv, a_part_recv, b_send, b_recv,
    l_send, l_recv, ps_sem, pr_sem, rs_sem, rr_sem, pq_send, pq_recv,
    qs_sem, qr_sem, ts_sem, tr_sem, zs_sem, zr_sem,
):
    rows, width = feats_ref.shape
    inputs = [
        pltpu.make_async_copy(src, dst, in_sem.at[i])
        for i, (src, dst) in enumerate((
            (text_hbm, text_ref), (feats_hbm, feats_ref), (w_hbm, wv), (scale_hbm, scale_ref), (shift_hbm, shift_ref),
        ))
    ]
    for copy in inputs:
        copy.start()
    chunk = 16
    n_chunk = rows // chunk
    wide = lax.axis_index("wide")
    narrow = lax.axis_index("narrow")
    x = wide % NX
    z = (wide // NX) % NZ
    y = (wide // (NX * NZ)) * 2 + narrow // 2
    core = narrow % 2

    def dev(dx=0, dy=0, dz=0, other=False):
        tx = (x + dx) % NX
        ty = (y + dy) % NY
        tz = (z + dz) % NZ
        tc = (1 - core) if other else core
        return ((ty // 2) * (NX * NZ) + tz * NX + tx, (ty % 2) * 2 + tc)

    def dev_b(dp, dq):
        return dev(dx=dp * (1 - core) + dq * core, dy=dp * core + dq * (1 - core))

    step_z = 1 + core * (NZ - 2)
    along = dev(dz=step_z)
    against = dev(dz=NZ - step_z)
    partner = dev(other=True)

    def rcopy(src, dst, ssem, rsem, target):
        return pltpu.make_async_remote_copy(
            src_ref=src, dst_ref=dst, send_sem=ssem, recv_sem=rsem,
            device_id=target, device_id_type=MESH,
        )

    sends = []

    def send(src, dst, ssem, rsem, target, keep=True):
        copy = rcopy(src, dst, ssem, rsem, target)
        copy.start()
        if keep:
            sends.append(copy)

    def sent(part_of, ssem):
        rcopy(part_of, part_of, ssem, ssem, partner).wait_send()

    def arrived(dst, rsem):
        rcopy(dst, dst, rsem, rsem, partner).wait_recv()

    barrier = pltpu.get_barrier_semaphore()
    peers = [dev_b(dp, dq) for dp in range(4) for dq in range(4) if (dp, dq) != (0, 0)]
    peers += [dev(dz=dz) for dz in range(1, 8)] + [partner]
    for peer in peers:
        pl.semaphore_signal(barrier, inc=1, device_id=peer, device_id_type=MESH)

    def a_part(slot, c):
        return ta.at[pl.ds(SLOT_ROW[slot] * rows + c * chunk, chunk)]

    def a_copy(name, c, to_name, target):
        i = STREAM.index(to_name)
        send(a_part(("O", name), c), a_part(("O", to_name), c), a_send, a_ring_recv.at[i, c], target, keep=False)

    def a_hand(name, c):
        i = STREAM.index(name)
        send(a_part(("O", name), c), a_part(("X", name), c), a_send, a_part_recv.at[i, c], partner, keep=False)

    def a_start():
        for c in range(n_chunk):
            a_copy("0", c, "L1", along)
            a_copy("0", c, "S1", against)
            a_hand("0", c)

    def a_wait(name, c):
        arrived(a_part(("O", name), c), a_ring_recv.at[STREAM.index(name), c])

    def a_step(n):
        for c in range(n_chunk):
            a_wait(f"L{n}", c)
            if n < 4:
                a_copy(f"L{n}", c, f"L{n + 1}", along)
            a_hand(f"L{n}", c)
            if n <= 3:
                a_wait(f"S{n}", c)
                if n < 3:
                    a_copy(f"S{n}", c, f"S{n + 1}", against)
                a_hand(f"S{n}", c)

    def a_finish(*names):
        for name in names:
            for c in range(n_chunk):
                arrived(a_part(("X", name), c), a_part_recv.at[STREAM.index(name), c])

    class Plane:
        def __init__(self, buf, ssem, rsem, size):
            self.buf, self.ssem, self.rsem, self.size = buf, ssem, rsem, size

        def part(self, dp, dq, c):
            return self.buf.at[pl.ds((ROW_OF_DQ[dq % 4] * 4 + dp % 4) * rows + c * self.size, self.size)]

        def copy(self, dp, dq, mp, mq, c):
            to = ((dp - mp) % 4, (dq - mq) % 4)
            send(
                self.part(dp, dq, c), self.part(*to, c), self.ssem, self.rsem.at[to[1] * 4 + to[0], c],
                dev_b(mp % 4, mq % 4), keep=False,
            )

        def wait(self, dp, dq, c):
            arrived(self.part(dp, dq, c), self.rsem.at[dq * 4 + dp, c])

        def spread(self, dp, c):
            self.copy(dp, 0, 0, 1, c)
            self.copy(dp, 0, 0, -1, c)

        def start(self, c):
            self.copy(0, 0, 1, 0, c)
            self.copy(0, 0, -1, 0, c)
            self.spread(0, c)

        def first(self, c):
            self.wait(3, 0, c)
            self.copy(3, 0, 1, 0, c)
            self.spread(3, c)
            self.wait(1, 0, c)
            self.spread(1, c)
            self.wait(0, 1, c)
            self.copy(0, 1, 0, -1, c)

        def second(self, c):
            self.wait(2, 0, c)
            self.spread(2, c)
            self.wait(3, 3, c)
            self.copy(3, 3, 0, 1, c)
            self.wait(1, 1, c)
            self.copy(1, 1, 0, -1, c)

        def third(self, c):
            self.wait(2, 3, c)
            self.copy(2, 3, 0, 1, c)
            self.wait(0, 3, c)
            self.wait(1, 3, c)

        def fourth(self, c):
            self.wait(3, 1, c)
            self.wait(2, 1, c)

        def last(self, c):
            for dp, dq in ((0, 2), (3, 2), (1, 2), (2, 2)):
                self.wait(dp, dq, c)

        def run(self, step):
            for c in range(rows // self.size):
                step(c)

    images = Plane(fb, b_send, b_recv, chunk)

    inputs[0].wait()
    text = text_ref[...].astype(F32)
    text_inv = lax.rsqrt(jnp.sum(text * text, axis=1, keepdims=True) + 1e-06)
    own_a = SLOT_ROW[("O", "0")] * rows
    own_b = ROW_OF_DQ[0] * 4 * rows
    ta[own_a : own_a + rows] = (text * text_inv).astype(BF16)

    col = lax.broadcasted_iota(jnp.int32, (width, 128), 0)
    combo = (col * 911) >> 17
    rest = col - 144 * combo
    layer = (rest * 3641) >> 16
    source = 18 * (32 * (combo >> 2) + 4 * layer + (combo & 3)) + rest - 18 * layer
    lane = lax.broadcasted_iota(jnp.int32, (width, 128), 1)
    for j in range(width // 128):
        order[:, 128 * j : 128 * (j + 1)] = jnp.where(source == lane + 128 * j, 1.0, 0.0).astype(BF16)
    inputs[1].wait()
    fb[own_b : own_b + rows] = lax.dot_general(
        feats_ref[...], order[...], (((1,), (1,)), ((), ())), preferred_element_type=F32
    ).astype(BF16)
    zs[...] = jnp.zeros_like(zs)
    loss_send[...] = jnp.zeros_like(loss_send)

    def weight(b):
        r = slice(384 * b, 384 * (b + 1))
        wp[r, :] = jnp.dot(order[r, :], wv[...], preferred_element_type=F32).astype(BF16)

    for copy in inputs[2:]:
        copy.wait()
    weight(0)
    pl.semaphore_wait(barrier, len(peers))
    a_start()
    images.run(images.start)
    weight(1)
    weight(2)

    quarter = 4 * rows

    def project(dq):
        r = slice(ROW_OF_DQ[dq] * quarter, (ROW_OF_DQ[dq] + 1) * quarter)
        zproj = jnp.dot(fb[r, :], wp[...], preferred_element_type=F32)
        img_inv = lax.rsqrt(jnp.sum(zproj * zproj, axis=1, keepdims=True) + 1e-06)
        ub[r, :] = (zproj * img_inv).astype(BF16)
        inv[r, :] = jnp.broadcast_to(img_inv, (quarter, 128))

    scale = jnp.exp(jnp.full((1, 128), scale_ref[0], F32))[:, :1]
    shift = shift_ref[0]
    half = 8 * rows

    def cell(batch, pair):
        r0, r1 = (rows * b for b in BATCHES[batch])
        prod = lax.dot_general(
            ta[r0:r1, :], ub[pair * half : (pair + 1) * half, :], (((1,), (1,)), ((), ())),
            preferred_element_type=F32,
        )
        for j in range(half // 128):
            lanes = slice(128 * j, 128 * (j + 1))
            logit = scale * prod[:, lanes] + shift
            factor = scale
            if j == 0 and pair == 1 and r1 > own_a:
                row = lax.broadcasted_iota(jnp.int32, logit.shape, 0) + (r0 - own_a)
                own = row == lax.broadcasted_iota(jnp.int32, logit.shape, 1)
                logit = jnp.where(own, -logit, logit)
                factor = jnp.where(own, -scale, scale)
            e = jnp.exp(logit)
            g[pair, r0:r1, lanes] = (factor * (e / (1.0 + e))).astype(BF16)
            total = jnp.sum(jnp.log1p(e).reshape((r1 - r0) // 8, 8, 128), axis=0)
            if batch == 2:
                loss_acc[pair, :, lanes] = total
            else:
                loss_acc[pair, :, lanes] += total

    a_step(1)
    images.run(images.first)
    a_step(2)
    images.run(images.second)
    project(0)
    a_step(3)
    images.run(images.third)
    project(3)
    a_step(4)
    images.run(images.fourth)
    a_finish("0", "L1", "S1")
    cell(2, 1)
    project(1)
    a_finish("L2", "S2")
    cell(1, 1)
    images.run(images.last)
    project(2)
    cell(2, 0)
    cell(1, 0)
    a_finish("L3", "S3", "L4")
    cell(0, 1)
    cell(0, 0)

    def image_half(pair):
        r = slice(pair * half, (pair + 1) * half)
        d = lax.dot_general(g[pair], ta[...], (((0,), (0,)), ((), ())), preferred_element_type=F32)
        u = ub[r, :].astype(F32)
        dzb[r, :] = (inv[r, :1] * (d - u * jnp.sum(u * d, axis=1, keepdims=True))).astype(BF16)

    for pair in range(2):
        summed = jnp.sum(loss_acc[pair], axis=0, keepdims=True)
        for k in range(8):
            loss_send[8 * pair + k, :1, :rows] = summed[:, k * rows : (k + 1) * rows]
    for dq in range(4):
        for dp in range(4):
            if (dp, dq) != (0, 0):
                i = ((4 - dq) % 4) * 4 + (4 - dp) % 4
                k = ROW_OF_DQ[dq] * 4 + dp
                send(loss_send.at[k], loss_recv.at[i], l_send, l_recv.at[i], dev_b(dp, dq), keep=False)

    image_half(1)
    image_half(0)

    block = 384
    for b in range(width // block):
        r = slice(b * block, (b + 1) * block)
        out = lax.dot_general(fb[:, r], dzb[...], (((0,), (0,)), ((), ())), preferred_element_type=F32)
        qf[r, :] = out
        qb[r, :] = out.astype(BF16)
        for yl in range(2):
            lanes = pl.ds(pl.multiple_of(256 * (1 - core) + 512 * yl, 128), 384)
            send(qb.at[r, lanes], pq.at[yl, r], pq_send.at[b, yl], pq_recv.at[b, yl], partner)

    def slot_rows(slot, c=None):
        if c is None:
            return pl.ds(SLOT_ROW[slot] * rows, rows)
        return pl.ds(SLOT_ROW[slot] * rows + c * chunk, chunk)

    def text_batch(b):
        lo, hi = BATCHES[b]
        r = slice(lo * rows, hi * rows)
        acc = jnp.dot(g[0, r, :], ub[:half], preferred_element_type=F32)
        acc += jnp.dot(g[1, r, :], ub[half:], preferred_element_type=F32)
        d_text[r, :] = acc
        for kind, name in SLOTS[lo:hi]:
            if kind == "X":
                i = STREAM.index(name)
                psend[i] = d_text[slot_rows((kind, name)), :].astype(BF16)
                send(psend.at[i], precv.at[i], ps_sem.at[i], pr_sem.at[i], partner)

    def handed(name):
        i = STREAM.index(name)
        arrived(precv.at[i], pr_sem.at[i])

    def gathered(name, c):
        r = slice(c * chunk, (c + 1) * chunk)
        value = d_text[slot_rows(("O", name), c), :] + precv[STREAM.index(name), r].astype(F32)
        if name == "0":
            before = ["L1", "S1"]
        elif name in ("L4", "S3"):
            before = []
        else:
            before = [name[0] + str(int(name[1]) + 1)]
        for prev in before:
            j = RING.index(prev)
            arrived(rrecv.at[j, r], rr_sem.at[j, c])
            value = value + rrecv[j, r].astype(F32)
        return value

    def ring(*names):
        for name in names:
            handed(name)
        for c in range(n_chunk):
            r = slice(c * chunk, (c + 1) * chunk)
            for name in names:
                i = RING.index(name)
                rsend[i, r] = gathered(name, c).astype(BF16)
                send(
                    rsend.at[i, r], rrecv.at[i, r], rs_sem.at[i], rr_sem.at[i, c],
                    against if name[0] == "L" else along, keep=False,
                )

    def unit(dp, dq):
        px = (x + dp * (1 - core) + dq * core) % NX
        py = (y + dp * core + dq * (1 - core)) % NY
        r = pl.ds(pl.multiple_of(144 * ((py // 2) * NX + px), 16), 144)
        lanes = pl.ds(pl.multiple_of(256 * core + 512 * (py % 2), 128), 384)
        return qf[r, lanes] + pq[py % 2, r, :].astype(F32)

    text_batch(0)
    for b in range(width // block):
        for yl in range(2):
            arrived(pq.at[yl, pl.ds(b * block, block)], pq_recv.at[b, yl])
    for dp in (2, 1, 3, 0):
        for dq in (2, 1, 3):
            qs[dq - 1, dp] = unit(dp, dq).astype(BF16)
            send(
                qs.at[dq - 1, dp], qr.at[dq - 1, dp], qs_sem.at[dq - 1, dp], qr_sem.at[dq - 1, dp], dev_b(0, dq)
            )
    for dp in range(4):
        qo[dp] = unit(dp, 0)
    text_batch(1)
    ring("L4")
    text_batch(2)
    ring("L3", "S3")
    ring("L2", "S2")

    def mine(dp):
        total = qo[dp]
        for i in (0, 2, 1):
            arrived(qr.at[i, dp], qr_sem.at[i, dp])
            total = total + qr[i, dp].astype(F32)
        return total

    def plane(dp):
        ps[dp - 1] = mine(dp).astype(BF16)
        send(ps.at[dp - 1], pr.at[dp - 1], ts_sem.at[dp - 1], tr_sem.at[dp - 1], dev_b(dp, 0))

    plane(2)
    ring("L1", "S1")
    plane(1)
    plane(3)
    handed("0")
    for c in range(n_chunk):
        dtext_out[c * chunk : (c + 1) * chunk] = gathered("0", c)
    loss = loss_send[ROW_OF_DQ[0] * 4]
    for i in range(1, 16):
        arrived(loss_recv.at[i], l_recv.at[i])
        loss = loss + loss_recv[i]
    loss_out[...] = loss
    outputs = [
        pltpu.make_async_copy(src, dst, out_sem.at[i])
        for i, (src, dst) in enumerate(((loss_out, loss_hbm), (dtext_out, dtext_hbm), (dproj_out, dproj_hbm)))
    ]
    outputs[0].start()
    outputs[1].start()
    own = mine(0)
    for i in (0, 2, 1):
        arrived(pr.at[i], tr_sem.at[i])
        own = own + pr[i].astype(F32)
    fz[...] = own
    for tz in range(NZ):
        piece = fz[18 * tz : 18 * tz + 18, :]
        zf[tz, :18] = piece
        zs[tz, :18] = piece.astype(BF16)
    for dz in (4, 3, 5, 2, 6, 1, 7):
        send(zs.at[(z + dz) % NZ], zr.at[NZ - dz], zs_sem.at[dz], zr_sem.at[NZ - dz], dev(dz=dz))

    acc = zf[z, :18]
    for dz in range(1, 8):
        arrived(zr.at[dz], zr_sem.at[dz])
        acc = acc + zr[dz, :18].astype(F32)
    fin[:18] = acc
    for n in range(4):
        @pl.when(narrow == n)
        def _():
            dproj_out[...] = fin[:18, 32 * n : 32 * n + 288]

    outputs[2].start()
    for copy in sends:
        copy.wait_send()
    for i in range(7):
        sent(rsend.at[i], rs_sem.at[i])
    sent(ta.at[pl.ds(0, 15 * rows)], a_send)
    sent(fb.at[pl.ds(0, 15 * rows)], b_send)
    sent(loss_send.at[pl.ds(0, 15)], l_send)
    for copy in outputs:
        copy.wait()


def results(loss_ref, dtext_ref, dproj_ref, loss_out, dtext_out, dproj_out):
    loss_out[...] = loss_ref[:1, : loss_out.shape[1]]
    dtext_out[...] = dtext_ref[...]
    dproj_out[...] = dproj_ref[...]


def local(image_feats, proj_weight, text_embed, log_scale, logit_bias):
    rows, width = image_feats.shape
    vmem = pl.BlockSpec(memory_space=pltpu.VMEM)
    anywhere = pl.BlockSpec(memory_space=pl.ANY)
    group = 16 * rows
    dma = pltpu.SemaphoreType.DMA
    loss, d_text, d_proj = pl.pallas_call(
        kernel,
        out_shape=(
            jax.ShapeDtypeStruct((8, 128), F32),
            jax.ShapeDtypeStruct((rows, width), F32),
            jax.ShapeDtypeStruct((width // 64, width // 4), F32),
        ),
        in_specs=[anywhere] * 5,
        out_specs=(anywhere, anywhere, anywhere),
        scratch_shapes=[
            pltpu.SMEM((1,), F32),
            pltpu.SMEM((1,), F32),
            pltpu.VMEM((rows, width), BF16),
            pltpu.VMEM((rows, width), BF16),
            pltpu.VMEM((width, width), BF16),
            pltpu.VMEM((width, width), BF16),
            pltpu.VMEM((width, width), BF16),
            pltpu.VMEM((group, width), BF16),
            pltpu.VMEM((group, width), BF16),
            pltpu.VMEM((group, width), BF16),
            pltpu.VMEM((group, 128), F32),
            pltpu.VMEM((2, group, group // 2), BF16),
            pltpu.VMEM((2, 8, group // 2), F32),
            pltpu.VMEM((16, 8, 128), F32),
            pltpu.VMEM((16, 8, 128), F32),
            pltpu.VMEM((group, width), F32),
            pltpu.VMEM((8, rows, width), BF16),
            pltpu.VMEM((8, rows, width), BF16),
            pltpu.VMEM((7, rows, width), BF16),
            pltpu.VMEM((7, rows, width), BF16),
            pltpu.VMEM((group, width), BF16),
            pltpu.VMEM((width, width), F32),
            pltpu.VMEM((width, width), BF16),
            pltpu.VMEM((2, width, 384), BF16),
            pltpu.VMEM((3, 4, 144, 384), BF16),
            pltpu.VMEM((4, 144, 384), F32),
            pltpu.VMEM((3, 4, 144, 384), BF16),
            pltpu.VMEM((3, 144, 384), BF16),
            pltpu.VMEM((3, 144, 384), BF16),
            pltpu.VMEM((144, 384), F32),
            pltpu.VMEM((8, 24, 384), F32),
            pltpu.VMEM((8, 32, 384), BF16),
            pltpu.VMEM((8, 32, 384), BF16),
            pltpu.VMEM((24, 384), F32),
            pltpu.VMEM((8, 128), F32),
            pltpu.VMEM((rows, width), F32),
            pltpu.VMEM((width // 64, width // 4), F32),
            dma((5,)), dma((3,)), dma, dma((8, 3)), dma((8, 3)),
            dma, dma((16, 3)),
            dma, dma((16,)), dma((8,)), dma((8,)), dma((7,)), dma((7, 3)),
            dma((3, 2)), dma((3, 2)),
            dma((3, 4)), dma((3, 4)), dma((3,)), dma((3,)), dma((8,)), dma((8,)),
        ],
        compiler_params=pltpu.CompilerParams(
            collective_id=0, has_side_effects=True, vmem_limit_bytes=60 * 1024 * 1024
        ),
    )(log_scale, logit_bias, image_feats, proj_weight, text_embed)
    loss, d_text, d_proj = pl.pallas_call(
        results,
        out_shape=(
            jax.ShapeDtypeStruct((1, rows), F32),
            jax.ShapeDtypeStruct(d_text.shape, F32),
            jax.ShapeDtypeStruct(d_proj.shape, F32),
        ),
        in_specs=[vmem, vmem, vmem],
        out_specs=(vmem, vmem, vmem),
    )(loss, d_text, d_proj)
    return loss.reshape(rows), d_text, d_proj


def solution(mesh):
    placed = (P(("wide", "narrow"), None), P(), P(("wide", "narrow"), None), P(), P())
    return jax.shard_map(
        local,
        mesh=mesh,
        in_specs=placed,
        out_specs=(P(("wide", "narrow")), P(("wide", "narrow"), None), P("wide", "narrow")),
        check_vma=False,
    )
```

```python
import functools

import jax
import jax.numpy as jnp
from jax import lax
from jax.experimental import pallas as pl
from jax.experimental.pallas import tpu as pltpu
from jax.sharding import PartitionSpec as P

MESH = pl.DeviceIdType.MESH
F32 = jnp.float32
BF16 = jnp.bfloat16

NX, NY, NZ = 4, 4, 8
STREAM = ("L4", "L3", "S3", "L2", "S2", "L1", "S1", "0")
SLOTS = (
    ("X", "L4"), ("X", "L3"), ("X", "S3"), ("O", "L4"), ("O", "L3"), ("O", "S3"),
    ("X", "L2"), ("X", "S2"), ("O", "L2"), ("O", "S2"),
    ("X", "L1"), ("X", "S1"), ("X", "0"), ("O", "L1"), ("O", "S1"), ("O", "0"),
)
SLOT_ROW = {name: i for i, name in enumerate(SLOTS)}
BATCHES = ((0, 6), (6, 10), (10, 16))
RING = STREAM[:7]
PLANE_SLOTS = (
    (3, 1), (1, 3), (0, 2), (2, 3), (2, 1), (3, 2), (1, 2), (2, 2),
    (0, 0), (3, 0), (1, 0), (0, 1), (0, 3), (2, 0), (3, 3), (1, 1),
)
PLANE_ROW = {slot: i for i, slot in enumerate(PLANE_SLOTS)}


def kernel(
    scale_hbm, shift_hbm, feats_hbm, w_hbm, text_hbm,
    loss_hbm, dtext_hbm, dproj_hbm,
    scale_ref, shift_ref, feats_ref, text_ref, wv, order, wp, ta, ub, fb, inv, g, loss_acc, loss_send, loss_recv,
    d_text, psend, precv, rsend, rrecv, dzb, qf, qb, pq, qs, qo, qr, ps, pr, fz, zf, zs, zr, ext, fin,
    loss_out, dtext_out, dproj_out,
    in_sem, out_sem, a_send, a_ring_recv, a_part_recv, b_send, b_recv,
    l_send, l_recv, ps_sem, pr_sem, rs_sem, rr_sem, pq_send, pq_recv,
    qs_sem, qr_sem, ts_sem, tr_sem, zs_sem, zr_sem,
):
    rows, width = feats_ref.shape
    inputs = [
        pltpu.make_async_copy(src, dst, in_sem.at[i])
        for i, (src, dst) in enumerate((
            (text_hbm, text_ref), (feats_hbm, feats_ref), (w_hbm, wv), (scale_hbm, scale_ref), (shift_hbm, shift_ref),
        ))
    ]
    for copy in inputs:
        copy.start()
    chunk = 16
    n_chunk = rows // chunk
    wide = lax.axis_index("wide")
    narrow = lax.axis_index("narrow")
    x = wide % NX
    z = (wide // NX) % NZ
    y = (wide // (NX * NZ)) * 2 + narrow // 2
    core = narrow % 2

    def dev(dx=0, dy=0, dz=0, other=False):
        tx = (x + dx) % NX
        ty = (y + dy) % NY
        tz = (z + dz) % NZ
        tc = (1 - core) if other else core
        return ((ty // 2) * (NX * NZ) + tz * NX + tx, (ty % 2) * 2 + tc)

    def dev_b(dp, dq):
        return dev(dx=dp * (1 - core) + dq * core, dy=dp * core + dq * (1 - core))

    step_z = 1 + core * (NZ - 2)
    along = dev(dz=step_z)
    against = dev(dz=NZ - step_z)
    partner = dev(other=True)

    def rcopy(src, dst, ssem, rsem, target):
        return pltpu.make_async_remote_copy(
            src_ref=src, dst_ref=dst, send_sem=ssem, recv_sem=rsem,
            device_id=target, device_id_type=MESH,
        )

    sends = []

    def send(src, dst, ssem, rsem, target, keep=True):
        copy = rcopy(src, dst, ssem, rsem, target)
        copy.start()
        if keep:
            sends.append(copy)

    def sent(part_of, ssem):
        rcopy(part_of, part_of, ssem, ssem, partner).wait_send()

    def arrived(dst, rsem):
        rcopy(dst, dst, rsem, rsem, partner).wait_recv()

    barrier = pltpu.get_barrier_semaphore()
    peers = [dev_b(1, 0), dev_b(3, 0), dev_b(0, 1), dev_b(0, 3), along, against, partner]
    for peer in peers:
        pl.semaphore_signal(barrier, inc=1, device_id=peer, device_id_type=MESH)

    def a_part(slot, c):
        return ta.at[pl.ds(SLOT_ROW[slot] * rows + c * chunk, chunk)]

    def a_copy(name, c, to_name, target):
        i = STREAM.index(to_name)
        send(a_part(("O", name), c), a_part(("O", to_name), c), a_send, a_ring_recv.at[i, c], target, keep=False)

    def a_hand(name, c):
        i = STREAM.index(name)
        send(a_part(("O", name), c), a_part(("X", name), c), a_send, a_part_recv.at[i], partner, keep=False)

    def a_start():
        for c in range(n_chunk):
            a_copy("0", c, "L1", along)
            a_copy("0", c, "S1", against)
            a_hand("0", c)

    def a_wait(name, c):
        arrived(a_part(("O", name), c), a_ring_recv.at[STREAM.index(name), c])

    def a_step(n):
        for c in range(n_chunk):
            a_wait(f"L{n}", c)
            if n < 4:
                a_copy(f"L{n}", c, f"L{n + 1}", along)
            a_hand(f"L{n}", c)
            if n <= 3:
                a_wait(f"S{n}", c)
                if n < 3:
                    a_copy(f"S{n}", c, f"S{n + 1}", against)
                a_hand(f"S{n}", c)

    def a_finish(*names):
        for name in names:
            arrived(ta.at[pl.ds(SLOT_ROW["X", name] * rows, rows)], a_part_recv.at[STREAM.index(name)])

    class Plane:
        def __init__(self, buf, ssem, rsem, size):
            self.buf, self.ssem, self.rsem, self.size = buf, ssem, rsem, size

        def part(self, dp, dq, c):
            return self.buf.at[pl.ds(PLANE_ROW[dp % 4, dq % 4] * rows + c * self.size, self.size)]

        def copy(self, dp, dq, mp, mq, c):
            to = ((dp - mp) % 4, (dq - mq) % 4)
            send(
                self.part(dp, dq, c), self.part(*to, c), self.ssem, self.rsem.at[to[1] * 4 + to[0], c],
                dev_b(mp % 4, mq % 4), keep=False,
            )

        def wait(self, dp, dq, c):
            arrived(self.part(dp, dq, c), self.rsem.at[dq * 4 + dp, c])

        def spread(self, dp, c):
            self.copy(dp, 0, 0, 1, c)
            self.copy(dp, 0, 0, -1, c)

        def start(self, c):
            self.copy(0, 0, 1, 0, c)
            self.copy(0, 0, -1, 0, c)
            self.spread(0, c)

        def first(self, c):
            self.wait(3, 0, c)
            self.copy(3, 0, 1, 0, c)
            self.spread(3, c)
            self.wait(1, 0, c)
            self.spread(1, c)
            self.wait(0, 1, c)
            self.copy(0, 1, 0, -1, c)

        def second(self, c):
            self.wait(2, 0, c)
            self.spread(2, c)
            self.wait(3, 3, c)
            self.copy(3, 3, 0, 1, c)
            self.wait(1, 1, c)
            self.copy(1, 1, 0, -1, c)

        def third(self, c):
            self.wait(2, 3, c)
            self.copy(2, 3, 0, 1, c)

        def last(self, *slots):
            for c in range(rows // self.size):
                for dp, dq in slots:
                    self.wait(dp, dq, c)

        def run(self, step):
            for c in range(rows // self.size):
                step(c)

    images = Plane(fb, b_send, b_recv, chunk)

    col = lax.broadcasted_iota(jnp.int32, (width, 128), 0)
    combo = (col * 911) >> 17
    rest = col - 144 * combo
    layer = (rest * 3641) >> 16
    source = 18 * (32 * (combo >> 2) + 4 * layer + (combo & 3)) + rest - 18 * layer
    lane = lax.broadcasted_iota(jnp.int32, (width, 128), 1)
    for j in range(width // 128):
        order[:, 128 * j : 128 * (j + 1)] = jnp.where(source == lane + 128 * j, 1.0, 0.0).astype(BF16)
    inputs[0].wait()
    text = text_ref[...].astype(F32)
    text_inv = lax.rsqrt(jnp.sum(text * text, axis=1, keepdims=True) + 1e-06)
    own_a = SLOT_ROW[("O", "0")] * rows
    own_b = PLANE_ROW[0, 0] * rows
    ta[own_a : own_a + rows] = (text * text_inv).astype(BF16)

    pl.semaphore_wait(barrier, len(peers))
    a_start()
    inputs[1].wait()
    fb[own_b : own_b + rows] = lax.dot_general(
        feats_ref[...], order[...], (((1,), (1,)), ((), ())), preferred_element_type=F32
    ).astype(BF16)
    images.run(images.start)
    zs[...] = jnp.zeros_like(zs)
    ext[...] = jnp.zeros_like(ext)
    loss_send[...] = jnp.zeros_like(loss_send)

    def weight(b):
        r = slice(384 * b, 384 * (b + 1))
        wp[r, :] = jnp.dot(order[r, :], wv[...], preferred_element_type=F32).astype(BF16)

    for copy in inputs[2:]:
        copy.wait()
    weight(0)
    weight(1)

    half = 8 * rows

    def project(lo, hi):
        r = slice(lo * rows, hi * rows)
        zproj = jnp.dot(fb[r, :], wp[...], preferred_element_type=F32)
        img_inv = lax.rsqrt(jnp.sum(zproj * zproj, axis=1, keepdims=True) + 1e-06)
        ub[r, :] = (zproj * img_inv).astype(BF16)
        inv[r, :] = jnp.broadcast_to(img_inv, ((hi - lo) * rows, 128))

    scale = jnp.exp(jnp.full((1, 128), scale_ref[0], F32))[:, :1]
    shift = shift_ref[0]
    def cell(batch, pair):
        r0, r1 = (rows * b for b in BATCHES[batch])
        prod = lax.dot_general(
            ta[r0:r1, :], ub[pair * half : (pair + 1) * half, :], (((1,), (1,)), ((), ())),
            preferred_element_type=F32,
        )
        for j in range(half // 128):
            lanes = slice(128 * j, 128 * (j + 1))
            logit = scale * prod[:, lanes] + shift
            factor = scale
            if j == 0 and pair == 1 and r1 > own_a:
                row = lax.broadcasted_iota(jnp.int32, logit.shape, 0) + (r0 - own_a)
                own = row == lax.broadcasted_iota(jnp.int32, logit.shape, 1)
                logit = jnp.where(own, -logit, logit)
                factor = jnp.where(own, -scale, scale)
            e = jnp.exp(logit)
            g[pair, r0:r1, lanes] = (factor * (e / (1.0 + e))).astype(BF16)
            total = jnp.sum(jnp.log1p(e).reshape((r1 - r0) // 8, 8, 128), axis=0)
            if batch == 2:
                loss_acc[pair, :, lanes] = total
            else:
                loss_acc[pair, :, lanes] += total

    images.run(images.first)
    a_step(1)
    weight(2)
    images.last((0, 3))
    project(8, 13)
    images.run(images.second)
    a_step(2)
    project(13, 16)
    a_finish("0", "L1", "S1")
    cell(2, 1)
    a_step(3)
    images.run(images.third)
    a_finish("L2", "S2")
    cell(1, 1)
    images.last((3, 1), (1, 3), (0, 2))
    project(0, 3)
    a_step(4)
    images.last((2, 1), (3, 2), (1, 2), (2, 2))
    project(3, 8)
    cell(2, 0)
    cell(1, 0)
    a_finish("L3", "S3", "L4")
    cell(0, 1)
    cell(0, 0)

    def image_half(pair):
        r = slice(pair * half, (pair + 1) * half)
        d = lax.dot_general(g[pair], ta[...], (((0,), (0,)), ((), ())), preferred_element_type=F32)
        u = ub[r, :].astype(F32)
        dzb[r, :] = (inv[r, :1] * (d - u * jnp.sum(u * d, axis=1, keepdims=True))).astype(BF16)

    for pair in range(2):
        summed = jnp.sum(loss_acc[pair], axis=0, keepdims=True)
        for k in range(8):
            loss_send[8 * pair + k, :1, :rows] = summed[:, k * rows : (k + 1) * rows]
    for k, (dp, dq) in enumerate(PLANE_SLOTS):
        if (dp, dq) != (0, 0):
            i = ((4 - dq) % 4) * 4 + (4 - dp) % 4
            send(loss_send.at[k], loss_recv.at[i], l_send, l_recv, dev_b(dp, dq), keep=False)

    image_half(1)
    image_half(0)

    block = 384
    for b in range(width // block):
        r = slice(b * block, (b + 1) * block)
        out = lax.dot_general(fb[:, r], dzb[...], (((0,), (0,)), ((), ())), preferred_element_type=F32)
        qf[r, :] = out
        qb[r, :] = out.astype(BF16)
        for yl in range(2):
            lanes = pl.ds(pl.multiple_of(256 * (1 - core) + 512 * yl, 128), 384)
            send(qb.at[r, lanes], pq.at[yl, r], pq_send, pq_recv, partner, keep=False)

    def slot_rows(slot, c=None):
        if c is None:
            return pl.ds(SLOT_ROW[slot] * rows, rows)
        return pl.ds(SLOT_ROW[slot] * rows + c * chunk, chunk)

    def text_batch(b):
        lo, hi = BATCHES[b]
        r = slice(lo * rows, hi * rows)
        acc = jnp.dot(g[0, r, :], ub[:half], preferred_element_type=F32)
        acc += jnp.dot(g[1, r, :], ub[half:], preferred_element_type=F32)
        d_text[r, :] = acc
        for kind, name in SLOTS[lo:hi]:
            if kind == "X":
                i = STREAM.index(name)
                psend[i] = d_text[slot_rows((kind, name)), :].astype(BF16)
                send(psend.at[i], precv.at[i], ps_sem, pr_sem.at[i], partner, keep=False)

    def handed(name):
        i = STREAM.index(name)
        arrived(precv.at[i], pr_sem.at[i])

    def gathered(name, c):
        r = slice(c * chunk, (c + 1) * chunk)
        value = d_text[slot_rows(("O", name), c), :] + precv[STREAM.index(name), r].astype(F32)
        if name == "0":
            before = ["L1", "S1"]
        elif name in ("L4", "S3"):
            before = []
        else:
            before = [name[0] + str(int(name[1]) + 1)]
        for prev in before:
            j = RING.index(prev)
            arrived(rrecv.at[j, r], rr_sem.at[j, c])
            value = value + rrecv[j, r].astype(F32)
        return value

    def ring(*names):
        for name in names:
            handed(name)
        for c in range(n_chunk):
            r = slice(c * chunk, (c + 1) * chunk)
            for name in names:
                i = RING.index(name)
                rsend[i, r] = gathered(name, c).astype(BF16)
                send(
                    rsend.at[i, r], rrecv.at[i, r], rs_sem, rr_sem.at[i, c],
                    against if name[0] == "L" else along, keep=False,
                )

    def unit(dp, dq):
        px = (x + dp * (1 - core) + dq * core) % NX
        py = (y + dp * core + dq * (1 - core)) % NY
        r = pl.ds(pl.multiple_of(144 * ((py // 2) * NX + px), 16), 144)
        lanes = pl.ds(pl.multiple_of(256 * core + 512 * (py % 2), 128), 384)
        return qf[r, lanes] + pq[py % 2, r, :].astype(F32)

    text_batch(0)
    arrived(pq, pq_recv)
    for dp in (2, 1, 3, 0):
        for dq in (2, 1, 3):
            qs[dq - 1, dp] = unit(dp, dq).astype(BF16)
            send(
                qs.at[dq - 1, dp], qr.at[dq - 1, dp], qs_sem, qr_sem.at[dq - 1, dp], dev_b(0, dq), keep=False,
            )
    for dp in range(4):
        qo[dp] = unit(dp, 0)
    text_batch(1)
    ring("L4")
    text_batch(2)
    ring("L3", "S3")

    def mine(dp):
        total = qo[dp]
        for i in (0, 2, 1):
            arrived(qr.at[i, dp], qr_sem.at[i, dp])
            total = total + qr[i, dp].astype(F32)
        return total

    def plane(dp):
        ps[dp - 1] = mine(dp).astype(BF16)
        send(ps.at[dp - 1], pr.at[dp - 1], ts_sem, tr_sem, dev_b(dp, 0), keep=False)

    plane(2)
    ring("L2", "S2")
    plane(1)
    plane(3)
    ring("L1", "S1")
    own = mine(0)
    arrived(pr, tr_sem)
    for i in (0, 2, 1):
        own = own + pr[i].astype(F32)
    fz[...] = own
    for tz in range(NZ):
        piece = fz[18 * tz : 18 * tz + 18, :]
        zf[tz, :18] = piece
        zs[tz, :, :384] = piece[:16].astype(BF16)
        for t in range(3):
            ext[2 * t : 2 * t + 2, :] = fz[18 * tz + 16 : 18 * tz + 18, 128 * t : 128 * (t + 1)]
        zs[tz, :, 384:] = ext[...].astype(BF16)
    for dz in (4, 3, 5, 2, 6, 1, 7):
        send(zs.at[(z + dz) % NZ], zr.at[NZ - dz], zs_sem, zr_sem, dev(dz=dz), keep=False)

    handed("0")
    for c in range(n_chunk):
        dtext_out[c * chunk : (c + 1) * chunk] = gathered("0", c)
    loss = loss_send[PLANE_ROW[0, 0]]
    arrived(loss_recv.at[pl.ds(1, 15)], l_recv)
    for i in range(1, 16):
        loss = loss + loss_recv[i]
    loss_out[...] = loss
    outputs = [
        pltpu.make_async_copy(src, dst, out_sem.at[i])
        for i, (src, dst) in enumerate(((loss_out, loss_hbm), (dtext_out, dtext_hbm), (dproj_out, dproj_hbm)))
    ]
    outputs[0].start()
    outputs[1].start()
    acc = jnp.zeros((16, 512), F32)
    arrived(zr.at[pl.ds(1, 7)], zr_sem)
    for dz in range(1, 8):
        acc = acc + zr[dz].astype(F32)
    fin[:16] = zf[z, :16] + acc[:, :384]
    for t in range(3):
        fin[16:18, 128 * t : 128 * (t + 1)] = zf[z, 16:18, 128 * t : 128 * (t + 1)] + acc[2 * t : 2 * t + 2, 384:]
    for n in range(4):
        @pl.when(narrow == n)
        def _():
            dproj_out[...] = fin[:18, 32 * n : 32 * n + 288]

    outputs[2].start()
    for copy in sends:
        copy.wait_send()
    for buf, ssem in ((rsend, rs_sem), (psend, ps_sem), (qs, qs_sem), (ps, ts_sem), (pq, pq_send)):
        sent(buf, ssem)
    sent(zs.at[pl.ds(0, 7)], zs_sem)
    sent(ta.at[pl.ds(0, 15 * rows)], a_send)
    sent(fb.at[pl.ds(0, 15 * rows)], b_send)
    sent(loss_send.at[pl.ds(0, 15)], l_send)
    for copy in outputs:
        copy.wait()


def results(loss_ref, dtext_ref, dproj_ref, loss_out, dtext_out, dproj_out):
    loss_out[...] = loss_ref[:1, : loss_out.shape[1]]
    dtext_out[...] = dtext_ref[...]
    dproj_out[...] = dproj_ref[...]


def local(image_feats, proj_weight, text_embed, log_scale, logit_bias):
    rows, width = image_feats.shape
    vmem = pl.BlockSpec(memory_space=pltpu.VMEM)
    anywhere = pl.BlockSpec(memory_space=pl.ANY)
    group = 16 * rows
    dma = pltpu.SemaphoreType.DMA
    loss, d_text, d_proj = pl.pallas_call(
        kernel,
        out_shape=(
            jax.ShapeDtypeStruct((8, 128), F32),
            jax.ShapeDtypeStruct((rows, width), F32),
            jax.ShapeDtypeStruct((width // 64, width // 4), F32),
        ),
        in_specs=[pl.BlockSpec(memory_space=pltpu.HBM)] * 5,
        out_specs=(anywhere, anywhere, anywhere),
        scratch_shapes=[
            pltpu.SMEM((1,), F32),
            pltpu.SMEM((1,), F32),
            pltpu.VMEM((rows, width), BF16),
            pltpu.VMEM((rows, width), BF16),
            pltpu.VMEM((width, width), BF16),
            pltpu.VMEM((width, width), BF16),
            pltpu.VMEM((width, width), BF16),
            pltpu.VMEM((group, width), BF16),
            pltpu.VMEM((group, width), BF16),
            pltpu.VMEM((group, width), BF16),
            pltpu.VMEM((group, 128), F32),
            pltpu.VMEM((2, group, group // 2), BF16),
            pltpu.VMEM((2, 8, group // 2), F32),
            pltpu.VMEM((16, 8, 128), F32),
            pltpu.VMEM((16, 8, 128), F32),
            pltpu.VMEM((group, width), F32),
            pltpu.VMEM((8, rows, width), BF16),
            pltpu.VMEM((8, rows, width), BF16),
            pltpu.VMEM((7, rows, width), BF16),
            pltpu.VMEM((7, rows, width), BF16),
            pltpu.VMEM((group, width), BF16),
            pltpu.VMEM((width, width), F32),
            pltpu.VMEM((width, width), BF16),
            pltpu.VMEM((2, width, 384), BF16),
            pltpu.VMEM((3, 4, 144, 384), BF16),
            pltpu.VMEM((4, 144, 384), F32),
            pltpu.VMEM((3, 4, 144, 384), BF16),
            pltpu.VMEM((3, 144, 384), BF16),
            pltpu.VMEM((3, 144, 384), BF16),
            pltpu.VMEM((144, 384), F32),
            pltpu.VMEM((8, 24, 384), F32),
            pltpu.VMEM((8, 16, 512), BF16),
            pltpu.VMEM((8, 16, 512), BF16),
            pltpu.VMEM((16, 128), F32),
            pltpu.VMEM((24, 384), F32),
            pltpu.VMEM((8, 128), F32),
            pltpu.VMEM((rows, width), F32),
            pltpu.VMEM((width // 64, width // 4), F32),
            dma((5,)), dma((3,)), dma, dma((8, 3)), dma((8,)),
            dma, dma((16, 3)),
            dma, dma, dma, dma((8,)), dma, dma((7, 3)),
            dma, dma,
            dma, dma((3, 4)), dma, dma, dma, dma,
        ],
        compiler_params=pltpu.CompilerParams(
            collective_id=0, has_side_effects=True, vmem_limit_bytes=60 * 1024 * 1024
        ),
    )(log_scale, logit_bias, image_feats, proj_weight, text_embed)
    loss, d_text, d_proj = pl.pallas_call(
        results,
        out_shape=(
            jax.ShapeDtypeStruct((1, rows), F32),
            jax.ShapeDtypeStruct(d_text.shape, F32),
            jax.ShapeDtypeStruct(d_proj.shape, F32),
        ),
        in_specs=[vmem, vmem, vmem],
        out_specs=(vmem, vmem, vmem),
    )(loss, d_text, d_proj)
    return loss.reshape(rows), d_text, d_proj


def solution(mesh):
    placed = (P(("wide", "narrow"), None), P(), P(("wide", "narrow"), None), P(), P())
    return jax.shard_map(
        local,
        mesh=mesh,
        in_specs=placed,
        out_specs=(P(("wide", "narrow")), P(("wide", "narrow"), None), P("wide", "narrow")),
        check_vma=False,
    )
```

```python
import functools

import jax
import jax.numpy as jnp
from jax import lax
from jax.experimental import pallas as pl
from jax.experimental.pallas import tpu as pltpu
from jax.sharding import PartitionSpec as P

MESH = pl.DeviceIdType.MESH
F32 = jnp.float32
BF16 = jnp.bfloat16

NX, NY, NZ = 4, 4, 8
STREAM = ("L4", "L3", "S3", "L2", "S2", "L1", "S1", "0")
SLOTS = (
    ("X", "L4"), ("X", "L3"), ("X", "S3"), ("O", "L4"), ("O", "L3"), ("O", "S3"),
    ("X", "L2"), ("X", "S2"), ("O", "L2"), ("O", "S2"),
    ("X", "L1"), ("X", "S1"), ("X", "0"), ("O", "L1"), ("O", "S1"), ("O", "0"),
)
SLOT_ROW = {name: i for i, name in enumerate(SLOTS)}
BATCHES = ((0, 6), (6, 10), (10, 16))
RING = STREAM[:7]
PLANE_SLOTS = (
    (3, 1), (1, 3), (0, 2), (2, 3), (2, 1), (3, 2), (1, 2), (2, 2),
    (0, 0), (3, 0), (1, 0), (0, 1), (0, 3), (2, 0), (3, 3), (1, 1),
)
PLANE_ROW = {slot: i for i, slot in enumerate(PLANE_SLOTS)}


def kernel(
    scale_hbm, shift_hbm, feats_hbm, w_hbm, text_hbm,
    loss_hbm, dtext_hbm, dproj_hbm,
    scale_ref, shift_ref, feats_ref, text_ref, wv, order, wp, ta, ub, fb, inv, g, loss_acc, loss_send, loss_recv,
    d_text, psend, precv, rsend, rrecv, dzb, qf, qb, pq, qs, qo, qr, ps, pr, fz, zf, zs, zr, ext, fin,
    loss_out, dtext_out, dproj_out,
    in_sem, out_sem, a_send, a_ring_recv, a_part_recv, b_send, b_recv,
    l_send, l_recv, ps_sem, pr_sem, rs_sem, rr_sem, pq_send, pq_recv,
    qs_sem, qr_sem, ts_sem, tr_sem, zs_sem, zr_sem,
):
    rows, width = feats_ref.shape
    inputs = [
        pltpu.make_async_copy(src, dst, in_sem.at[i])
        for i, (src, dst) in enumerate((
            (text_hbm, text_ref), (feats_hbm, feats_ref), (w_hbm, wv), (scale_hbm, scale_ref), (shift_hbm, shift_ref),
        ))
    ]
    for copy in inputs:
        copy.start()
    chunk = 16
    n_chunk = rows // chunk
    wide = lax.axis_index("wide")
    narrow = lax.axis_index("narrow")
    x = wide % NX
    z = (wide // NX) % NZ
    y = (wide // (NX * NZ)) * 2 + narrow // 2
    core = narrow % 2

    def dev(dx=0, dy=0, dz=0, other=False):
        tx = (x + dx) % NX
        ty = (y + dy) % NY
        tz = (z + dz) % NZ
        tc = (1 - core) if other else core
        return ((ty // 2) * (NX * NZ) + tz * NX + tx, (ty % 2) * 2 + tc)

    def dev_b(dp, dq):
        return dev(dx=dp * (1 - core) + dq * core, dy=dp * core + dq * (1 - core))

    step_z = 1 + core * (NZ - 2)
    along = dev(dz=step_z)
    against = dev(dz=NZ - step_z)
    partner = dev(other=True)

    def rcopy(src, dst, ssem, rsem, target):
        return pltpu.make_async_remote_copy(
            src_ref=src, dst_ref=dst, send_sem=ssem, recv_sem=rsem,
            device_id=target, device_id_type=MESH,
        )

    sends = []

    def send(src, dst, ssem, rsem, target, keep=True):
        copy = rcopy(src, dst, ssem, rsem, target)
        copy.start()
        if keep:
            sends.append(copy)

    def sent(part_of, ssem):
        rcopy(part_of, part_of, ssem, ssem, partner).wait_send()

    def arrived(dst, rsem):
        rcopy(dst, dst, rsem, rsem, partner).wait_recv()

    barrier = pltpu.get_barrier_semaphore()
    peers = [dev_b(1, 0), dev_b(3, 0), dev_b(0, 1), dev_b(0, 3), along, against, partner]
    for peer in peers:
        pl.semaphore_signal(barrier, inc=1, device_id=peer, device_id_type=MESH)

    def a_part(slot, c):
        return ta.at[pl.ds(SLOT_ROW[slot] * rows + c * chunk, chunk)]

    def a_copy(name, c, to_name, target):
        i = STREAM.index(to_name)
        send(a_part(("O", name), c), a_part(("O", to_name), c), a_send, a_ring_recv.at[i, c], target, keep=False)

    def a_hand(name, c):
        i = STREAM.index(name)
        send(a_part(("O", name), c), a_part(("X", name), c), a_send, a_part_recv.at[i], partner, keep=False)

    def a_start():
        for c in range(n_chunk):
            a_copy("0", c, "L1", along)
            a_copy("0", c, "S1", against)
            a_hand("0", c)

    def a_wait(name, c):
        arrived(a_part(("O", name), c), a_ring_recv.at[STREAM.index(name), c])

    def a_step(n):
        for c in range(n_chunk):
            a_wait(f"L{n}", c)
            if n < 4:
                a_copy(f"L{n}", c, f"L{n + 1}", along)
            a_hand(f"L{n}", c)
            if n <= 3:
                a_wait(f"S{n}", c)
                if n < 3:
                    a_copy(f"S{n}", c, f"S{n + 1}", against)
                a_hand(f"S{n}", c)

    def a_finish(*names):
        for name in names:
            arrived(ta.at[pl.ds(SLOT_ROW["X", name] * rows, rows)], a_part_recv.at[STREAM.index(name)])

    class Plane:
        def __init__(self, buf, ssem, rsem, size):
            self.buf, self.ssem, self.rsem, self.size = buf, ssem, rsem, size

        def part(self, dp, dq, c):
            return self.buf.at[pl.ds(PLANE_ROW[dp % 4, dq % 4] * rows + c * self.size, self.size)]

        def copy(self, dp, dq, mp, mq, c):
            to = ((dp - mp) % 4, (dq - mq) % 4)
            send(
                self.part(dp, dq, c), self.part(*to, c), self.ssem, self.rsem.at[to[1] * 4 + to[0], c],
                dev_b(mp % 4, mq % 4), keep=False,
            )

        def wait(self, dp, dq, c):
            arrived(self.part(dp, dq, c), self.rsem.at[dq * 4 + dp, c])

        def spread(self, dp, c):
            self.copy(dp, 0, 0, 1, c)
            self.copy(dp, 0, 0, -1, c)

        def start(self, c):
            self.copy(0, 0, 1, 0, c)
            self.copy(0, 0, -1, 0, c)
            self.spread(0, c)

        def first(self, c):
            self.wait(3, 0, c)
            self.copy(3, 0, 1, 0, c)
            self.spread(3, c)
            self.wait(1, 0, c)
            self.spread(1, c)
            self.wait(0, 1, c)
            self.copy(0, 1, 0, -1, c)

        def second(self, c):
            self.wait(2, 0, c)
            self.spread(2, c)
            self.wait(3, 3, c)
            self.copy(3, 3, 0, 1, c)
            self.wait(1, 1, c)
            self.copy(1, 1, 0, -1, c)

        def third(self, c):
            self.wait(2, 3, c)
            self.copy(2, 3, 0, 1, c)

        def last(self, *slots):
            for c in range(rows // self.size):
                for dp, dq in slots:
                    self.wait(dp, dq, c)

        def run(self, step):
            for c in range(rows // self.size):
                step(c)

    images = Plane(fb, b_send, b_recv, chunk)

    col = lax.broadcasted_iota(jnp.int32, (width, 128), 0)
    combo = (col * 911) >> 17
    rest = col - 144 * combo
    layer = (rest * 3641) >> 16
    source = 18 * (32 * (combo >> 2) + 4 * layer + (combo & 3)) + rest - 18 * layer
    lane = lax.broadcasted_iota(jnp.int32, (width, 128), 1)
    for j in range(width // 128):
        order[:, 128 * j : 128 * (j + 1)] = jnp.where(source == lane + 128 * j, 1.0, 0.0).astype(BF16)
    inputs[0].wait()
    text = text_ref[...].astype(F32)
    text_inv = lax.rsqrt(jnp.sum(text * text, axis=1, keepdims=True) + 1e-06)
    own_a = SLOT_ROW[("O", "0")] * rows
    own_b = PLANE_ROW[0, 0] * rows
    ta[own_a : own_a + rows] = (text * text_inv).astype(BF16)

    pl.semaphore_wait(barrier, len(peers))
    a_start()
    inputs[1].wait()
    fb[own_b : own_b + rows] = lax.dot_general(
        feats_ref[...], order[...], (((1,), (1,)), ((), ())), preferred_element_type=F32
    ).astype(BF16)
    images.run(images.start)
    zs[...] = jnp.zeros_like(zs)
    ext[...] = jnp.zeros_like(ext)
    loss_send[...] = jnp.zeros_like(loss_send)

    def weight(b):
        r = slice(384 * b, 384 * (b + 1))
        wp[r, :] = jnp.dot(order[r, :], wv[...], preferred_element_type=F32).astype(BF16)

    for copy in inputs[2:]:
        copy.wait()
    weight(0)
    weight(1)

    half = 8 * rows

    def project(lo, hi):
        r = slice(lo * rows, hi * rows)
        zproj = jnp.dot(fb[r, :], wp[...], preferred_element_type=F32)
        img_inv = lax.rsqrt(jnp.sum(zproj * zproj, axis=1, keepdims=True) + 1e-06)
        ub[r, :] = (zproj * img_inv).astype(BF16)
        inv[r, :] = jnp.broadcast_to(img_inv, ((hi - lo) * rows, 128))

    scale = jnp.exp(jnp.full((1, 128), scale_ref[0], F32))[:, :1]
    shift = shift_ref[0]
    def cell(batch, pair):
        r0, r1 = (rows * b for b in BATCHES[batch])
        prod = lax.dot_general(
            ta[r0:r1, :], ub[pair * half : (pair + 1) * half, :], (((1,), (1,)), ((), ())),
            preferred_element_type=F32,
        )
        for j in range(half // 128):
            lanes = slice(128 * j, 128 * (j + 1))
            logit = scale * prod[:, lanes] + shift
            factor = scale
            if j == 0 and pair == 1 and r1 > own_a:
                row = lax.broadcasted_iota(jnp.int32, logit.shape, 0) + (r0 - own_a)
                own = row == lax.broadcasted_iota(jnp.int32, logit.shape, 1)
                logit = jnp.where(own, -logit, logit)
                factor = jnp.where(own, -scale, scale)
            e = jnp.exp(logit)
            g[pair, r0:r1, lanes] = (factor * (e / (1.0 + e))).astype(BF16)
            total = jnp.sum(jnp.log1p(e).reshape((r1 - r0) // 8, 8, 128), axis=0)
            if batch == 2:
                loss_acc[pair, :, lanes] = total
            else:
                loss_acc[pair, :, lanes] += total

    def image_half(pair):
        r = slice(pair * half, (pair + 1) * half)
        d = lax.dot_general(g[pair], ta[...], (((0,), (0,)), ((), ())), preferred_element_type=F32)
        u = ub[r, :].astype(F32)
        dzb[r, :] = (inv[r, :1] * (d - u * jnp.sum(u * d, axis=1, keepdims=True))).astype(BF16)

    images.run(images.first)
    a_step(1)
    weight(2)
    a_step(2)
    images.last((0, 3))
    project(8, 13)
    images.run(images.second)
    a_step(3)
    project(13, 16)
    a_finish("0", "L1", "S1")
    cell(2, 1)
    images.run(images.third)
    a_finish("L2", "S2")
    cell(1, 1)
    a_step(4)
    images.last((3, 1), (1, 3), (0, 2))
    project(0, 3)
    a_finish("L3", "S3", "L4")
    cell(0, 1)
    image_half(1)
    images.last((2, 1), (3, 2), (1, 2), (2, 2))
    project(3, 8)
    cell(2, 0)
    cell(1, 0)
    cell(0, 0)
    image_half(0)

    block = 384
    for b in range(width // block):
        r = slice(b * block, (b + 1) * block)
        out = lax.dot_general(fb[:, r], dzb[...], (((0,), (0,)), ((), ())), preferred_element_type=F32)
        qf[r, :] = out
        qb[r, :] = out.astype(BF16)
        for yl in range(2):
            lanes = pl.ds(pl.multiple_of(256 * (1 - core) + 512 * yl, 128), 384)
            send(qb.at[r, lanes], pq.at[yl, r], pq_send, pq_recv, partner, keep=False)

    def slot_rows(slot, c=None):
        if c is None:
            return pl.ds(SLOT_ROW[slot] * rows, rows)
        return pl.ds(SLOT_ROW[slot] * rows + c * chunk, chunk)

    def text_batch(b):
        lo, hi = BATCHES[b]
        r = slice(lo * rows, hi * rows)
        acc = jnp.dot(g[0, r, :], ub[:half], preferred_element_type=F32)
        acc += jnp.dot(g[1, r, :], ub[half:], preferred_element_type=F32)
        d_text[r, :] = acc
        for kind, name in SLOTS[lo:hi]:
            if kind == "X":
                i = STREAM.index(name)
                psend[i] = d_text[slot_rows((kind, name)), :].astype(BF16)
                send(psend.at[i], precv.at[i], ps_sem, pr_sem.at[i], partner, keep=False)

    def handed(name):
        i = STREAM.index(name)
        arrived(precv.at[i], pr_sem.at[i])

    def gathered(name, c):
        r = slice(c * chunk, (c + 1) * chunk)
        value = d_text[slot_rows(("O", name), c), :] + precv[STREAM.index(name), r].astype(F32)
        if name == "0":
            before = ["L1", "S1"]
        elif name in ("L4", "S3"):
            before = []
        else:
            before = [name[0] + str(int(name[1]) + 1)]
        for prev in before:
            j = RING.index(prev)
            arrived(rrecv.at[j, r], rr_sem.at[j, c])
            value = value + rrecv[j, r].astype(F32)
        return value

    def ring(*names):
        for name in names:
            handed(name)
        for c in range(n_chunk):
            r = slice(c * chunk, (c + 1) * chunk)
            for name in names:
                i = RING.index(name)
                rsend[i, r] = gathered(name, c).astype(BF16)
                send(
                    rsend.at[i, r], rrecv.at[i, r], rs_sem, rr_sem.at[i, c],
                    against if name[0] == "L" else along, keep=False,
                )

    def unit(dp, dq):
        px = (x + dp * (1 - core) + dq * core) % NX
        py = (y + dp * core + dq * (1 - core)) % NY
        r = pl.ds(pl.multiple_of(144 * ((py // 2) * NX + px), 16), 144)
        lanes = pl.ds(pl.multiple_of(256 * core + 512 * (py % 2), 128), 384)
        return qf[r, lanes] + pq[py % 2, r, :].astype(F32)

    text_batch(0)
    arrived(pq, pq_recv)
    for dp in (2, 1, 3, 0):
        for dq in (2, 1, 3):
            qs[dq - 1, dp] = unit(dp, dq).astype(BF16)
            send(
                qs.at[dq - 1, dp], qr.at[dq - 1, dp], qs_sem, qr_sem.at[dq - 1, dp], dev_b(0, dq), keep=False,
            )
    for dp in range(4):
        qo[dp] = unit(dp, 0)
    for pair in range(2):
        summed = jnp.sum(loss_acc[pair], axis=0, keepdims=True)
        for k in range(8):
            loss_send[8 * pair + k, :1, :rows] = summed[:, k * rows : (k + 1) * rows]
    for k, (dp, dq) in enumerate(PLANE_SLOTS):
        if (dp, dq) != (0, 0):
            i = ((4 - dq) % 4) * 4 + (4 - dp) % 4
            send(loss_send.at[k], loss_recv.at[i], l_send, l_recv, dev_b(dp, dq), keep=False)

    text_batch(1)
    ring("L4")
    text_batch(2)
    ring("L3", "S3")

    def mine(dp):
        total = qo[dp]
        for i in (0, 2, 1):
            arrived(qr.at[i, dp], qr_sem.at[i, dp])
            total = total + qr[i, dp].astype(F32)
        return total

    def plane(dp):
        ps[dp - 1] = mine(dp).astype(BF16)
        send(ps.at[dp - 1], pr.at[dp - 1], ts_sem, tr_sem, dev_b(dp, 0), keep=False)

    plane(2)
    ring("L2", "S2")
    plane(1)
    plane(3)
    ring("L1", "S1")
    own = mine(0)
    arrived(pr, tr_sem)
    for i in (0, 2, 1):
        own = own + pr[i].astype(F32)
    fz[...] = own
    for tz in range(NZ):
        piece = fz[18 * tz : 18 * tz + 18, :]
        zf[tz, :18] = piece
        zs[tz, :, :384] = piece[:16].astype(BF16)
        for t in range(3):
            ext[2 * t : 2 * t + 2, :] = fz[18 * tz + 16 : 18 * tz + 18, 128 * t : 128 * (t + 1)]
        zs[tz, :, 384:] = ext[...].astype(BF16)
    for dz in (4, 3, 5, 2, 6, 1, 7):
        send(zs.at[(z + dz) % NZ], zr.at[NZ - dz], zs_sem, zr_sem, dev(dz=dz), keep=False)

    handed("0")
    for c in range(n_chunk):
        dtext_out[c * chunk : (c + 1) * chunk] = gathered("0", c)
    loss = loss_send[PLANE_ROW[0, 0]]
    arrived(loss_recv.at[pl.ds(1, 15)], l_recv)
    for i in range(1, 16):
        loss = loss + loss_recv[i]
    loss_out[...] = loss
    outputs = [
        pltpu.make_async_copy(src, dst, out_sem.at[i])
        for i, (src, dst) in enumerate(((loss_out, loss_hbm), (dtext_out, dtext_hbm), (dproj_out, dproj_hbm)))
    ]
    outputs[0].start()
    outputs[1].start()
    acc = jnp.zeros((16, 512), F32)
    arrived(zr.at[pl.ds(1, 7)], zr_sem)
    for dz in range(1, 8):
        acc = acc + zr[dz].astype(F32)
    fin[:16] = zf[z, :16] + acc[:, :384]
    for t in range(3):
        fin[16:18, 128 * t : 128 * (t + 1)] = zf[z, 16:18, 128 * t : 128 * (t + 1)] + acc[2 * t : 2 * t + 2, 384:]
    for n in range(4):
        @pl.when(narrow == n)
        def _():
            dproj_out[...] = fin[:18, 32 * n : 32 * n + 288]

    outputs[2].start()
    for copy in sends:
        copy.wait_send()
    for buf, ssem in ((rsend, rs_sem), (psend, ps_sem), (qs, qs_sem), (ps, ts_sem), (pq, pq_send)):
        sent(buf, ssem)
    sent(zs.at[pl.ds(0, 7)], zs_sem)
    sent(ta.at[pl.ds(0, 15 * rows)], a_send)
    sent(fb.at[pl.ds(0, 15 * rows)], b_send)
    sent(loss_send.at[pl.ds(0, 15)], l_send)
    for copy in outputs:
        copy.wait()


def results(loss_ref, dtext_ref, dproj_ref, loss_out, dtext_out, dproj_out):
    loss_out[...] = loss_ref[:1, : loss_out.shape[1]]
    dtext_out[...] = dtext_ref[...]
    dproj_out[...] = dproj_ref[...]


def local(image_feats, proj_weight, text_embed, log_scale, logit_bias):
    rows, width = image_feats.shape
    vmem = pl.BlockSpec(memory_space=pltpu.VMEM)
    anywhere = pl.BlockSpec(memory_space=pl.ANY)
    group = 16 * rows
    dma = pltpu.SemaphoreType.DMA
    loss, d_text, d_proj = pl.pallas_call(
        kernel,
        out_shape=(
            jax.ShapeDtypeStruct((8, 128), F32),
            jax.ShapeDtypeStruct((rows, width), F32),
            jax.ShapeDtypeStruct((width // 64, width // 4), F32),
        ),
        in_specs=[pl.BlockSpec(memory_space=pltpu.HBM)] * 5,
        out_specs=(anywhere, anywhere, anywhere),
        scratch_shapes=[
            pltpu.SMEM((1,), F32),
            pltpu.SMEM((1,), F32),
            pltpu.VMEM((rows, width), BF16),
            pltpu.VMEM((rows, width), BF16),
            pltpu.VMEM((width, width), BF16),
            pltpu.VMEM((width, width), BF16),
            pltpu.VMEM((width, width), BF16),
            pltpu.VMEM((group, width), BF16),
            pltpu.VMEM((group, width), BF16),
            pltpu.VMEM((group, width), BF16),
            pltpu.VMEM((group, 128), F32),
            pltpu.VMEM((2, group, group // 2), BF16),
            pltpu.VMEM((2, 8, group // 2), F32),
            pltpu.VMEM((16, 8, 128), F32),
            pltpu.VMEM((16, 8, 128), F32),
            pltpu.VMEM((group, width), F32),
            pltpu.VMEM((8, rows, width), BF16),
            pltpu.VMEM((8, rows, width), BF16),
            pltpu.VMEM((7, rows, width), BF16),
            pltpu.VMEM((7, rows, width), BF16),
            pltpu.VMEM((group, width), BF16),
            pltpu.VMEM((width, width), F32),
            pltpu.VMEM((width, width), BF16),
            pltpu.VMEM((2, width, 384), BF16),
            pltpu.VMEM((3, 4, 144, 384), BF16),
            pltpu.VMEM((4, 144, 384), F32),
            pltpu.VMEM((3, 4, 144, 384), BF16),
            pltpu.VMEM((3, 144, 384), BF16),
            pltpu.VMEM((3, 144, 384), BF16),
            pltpu.VMEM((144, 384), F32),
            pltpu.VMEM((8, 24, 384), F32),
            pltpu.VMEM((8, 16, 512), BF16),
            pltpu.VMEM((8, 16, 512), BF16),
            pltpu.VMEM((16, 128), F32),
            pltpu.VMEM((24, 384), F32),
            pltpu.VMEM((8, 128), F32),
            pltpu.VMEM((rows, width), F32),
            pltpu.VMEM((width // 64, width // 4), F32),
            dma((5,)), dma((3,)), dma, dma((8, 3)), dma((8,)),
            dma, dma((16, 3)),
            dma, dma, dma, dma((8,)), dma, dma((7, 3)),
            dma, dma,
            dma, dma((3, 4)), dma, dma, dma, dma,
        ],
        compiler_params=pltpu.CompilerParams(
            collective_id=0, has_side_effects=True, vmem_limit_bytes=60 * 1024 * 1024
        ),
    )(log_scale, logit_bias, image_feats, proj_weight, text_embed)
    loss, d_text, d_proj = pl.pallas_call(
        results,
        out_shape=(
            jax.ShapeDtypeStruct((1, rows), F32),
            jax.ShapeDtypeStruct(d_text.shape, F32),
            jax.ShapeDtypeStruct(d_proj.shape, F32),
        ),
        in_specs=[vmem, vmem, vmem],
        out_specs=(vmem, vmem, vmem),
    )(loss, d_text, d_proj)
    return loss.reshape(rows), d_text, d_proj


def solution(mesh):
    placed = (P(("wide", "narrow"), None), P(), P(("wide", "narrow"), None), P(), P())
    return jax.shard_map(
        local,
        mesh=mesh,
        in_specs=placed,
        out_specs=(P(("wide", "narrow")), P(("wide", "narrow"), None), P("wide", "narrow")),
        check_vma=False,
    )
```

```python
import functools

import jax
import jax.numpy as jnp
from jax import lax
from jax.experimental import pallas as pl
from jax.experimental.pallas import tpu as pltpu
from jax.sharding import PartitionSpec as P

MESH = pl.DeviceIdType.MESH
F32 = jnp.float32
BF16 = jnp.bfloat16

NX, NY, NZ = 4, 4, 8
STREAM = ("L4", "L3", "S3", "L2", "S2", "L1", "S1", "0")
SLOTS = (
    ("X", "L4"), ("X", "L3"), ("X", "S3"), ("O", "L4"), ("O", "L3"), ("O", "S3"),
    ("X", "L2"), ("X", "S2"), ("O", "L2"), ("O", "S2"),
    ("X", "L1"), ("X", "S1"), ("X", "0"), ("O", "L1"), ("O", "S1"), ("O", "0"),
)
SLOT_ROW = {name: i for i, name in enumerate(SLOTS)}
BATCHES = ((0, 6), (6, 10), (10, 16))
RING = STREAM[:7]
PLANE_SLOTS = (
    (3, 1), (1, 3), (0, 2), (2, 3), (2, 1), (3, 2), (1, 2), (2, 2),
    (0, 0), (3, 0), (1, 0), (0, 1), (0, 3), (2, 0), (3, 3), (1, 1),
)
PLANE_ROW = {slot: i for i, slot in enumerate(PLANE_SLOTS)}


def kernel(
    scale_hbm, shift_hbm, feats_hbm, w_hbm, text_hbm,
    loss_hbm, dtext_hbm, dproj_hbm,
    scale_ref, shift_ref, feats_ref, text_ref, wv, order, wp, ta, ub, fb, inv, g, loss_acc, loss_send, loss_recv,
    d_text, psend, precv, rsend, rrecv, dzb, qf, qb, pq, qs, qo, qr, ps, pr, fz, zf, zs, zr, ext, fin,
    loss_out, dtext_out, dproj_out,
    in_sem, out_sem, a_send, a_ring_recv, a_part_recv, b_send, b_recv,
    l_send, l_recv, ps_sem, pr_sem, rs_sem, rr_sem, pq_send, pq_recv,
    qs_sem, qr_sem, ts_sem, tr_sem, zs_sem, zr_sem,
):
    rows, width = feats_ref.shape
    inputs = [
        pltpu.make_async_copy(src, dst, in_sem.at[i])
        for i, (src, dst) in enumerate((
            (text_hbm, text_ref), (feats_hbm, feats_ref), (w_hbm, wv), (scale_hbm, scale_ref), (shift_hbm, shift_ref),
        ))
    ]
    for copy in inputs:
        copy.start()
    chunk = 16
    n_chunk = rows // chunk
    wide = lax.axis_index("wide")
    narrow = lax.axis_index("narrow")
    x = wide % NX
    z = (wide // NX) % NZ
    y = (wide // (NX * NZ)) * 2 + narrow // 2
    core = narrow % 2

    def dev(dx=0, dy=0, dz=0, other=False):
        tx = (x + dx) % NX
        ty = (y + dy) % NY
        tz = (z + dz) % NZ
        tc = (1 - core) if other else core
        return ((ty // 2) * (NX * NZ) + tz * NX + tx, (ty % 2) * 2 + tc)

    def dev_b(dp, dq):
        return dev(dx=dp * (1 - core) + dq * core, dy=dp * core + dq * (1 - core))

    step_z = 1 + core * (NZ - 2)
    along = dev(dz=step_z)
    against = dev(dz=NZ - step_z)
    partner = dev(other=True)

    def rcopy(src, dst, ssem, rsem, target):
        return pltpu.make_async_remote_copy(
            src_ref=src, dst_ref=dst, send_sem=ssem, recv_sem=rsem,
            device_id=target, device_id_type=MESH,
        )

    sends = []

    def send(src, dst, ssem, rsem, target, keep=True):
        copy = rcopy(src, dst, ssem, rsem, target)
        copy.start()
        if keep:
            sends.append(copy)

    def sent(part_of, ssem):
        rcopy(part_of, part_of, ssem, ssem, partner).wait_send()

    def arrived(dst, rsem):
        rcopy(dst, dst, rsem, rsem, partner).wait_recv()

    barrier = pltpu.get_barrier_semaphore()
    peers = [dev_b(1, 0), dev_b(3, 0), dev_b(0, 1), dev_b(0, 3), along, against, partner]
    for peer in peers:
        pl.semaphore_signal(barrier, inc=1, device_id=peer, device_id_type=MESH)

    def a_part(slot, c):
        return ta.at[pl.ds(SLOT_ROW[slot] * rows + c * chunk, chunk)]

    def a_copy(name, c, to_name, target):
        i = STREAM.index(to_name)
        send(a_part(("O", name), c), a_part(("O", to_name), c), a_send, a_ring_recv.at[i, c], target, keep=False)

    def a_hand(name, c):
        i = STREAM.index(name)
        send(a_part(("O", name), c), a_part(("X", name), c), a_send, a_part_recv.at[i], partner, keep=False)

    def a_start():
        for c in range(n_chunk):
            a_copy("0", c, "L1", along)
            a_copy("0", c, "S1", against)
            a_hand("0", c)

    def a_wait(name, c):
        arrived(a_part(("O", name), c), a_ring_recv.at[STREAM.index(name), c])

    def a_step(n):
        for c in range(n_chunk):
            a_wait(f"L{n}", c)
            if n < 4:
                a_copy(f"L{n}", c, f"L{n + 1}", along)
            a_hand(f"L{n}", c)
            if n <= 3:
                a_wait(f"S{n}", c)
                if n < 3:
                    a_copy(f"S{n}", c, f"S{n + 1}", against)
                a_hand(f"S{n}", c)

    def a_finish(*names):
        for name in names:
            arrived(ta.at[pl.ds(SLOT_ROW["X", name] * rows, rows)], a_part_recv.at[STREAM.index(name)])

    class Plane:
        def __init__(self, buf, ssem, rsem, size):
            self.buf, self.ssem, self.rsem, self.size = buf, ssem, rsem, size

        def part(self, dp, dq, c):
            return self.buf.at[pl.ds(PLANE_ROW[dp % 4, dq % 4] * rows + c * self.size, self.size)]

        def copy(self, dp, dq, mp, mq, c):
            to = ((dp - mp) % 4, (dq - mq) % 4)
            send(
                self.part(dp, dq, c), self.part(*to, c), self.ssem, self.rsem.at[to[1] * 4 + to[0], c],
                dev_b(mp % 4, mq % 4), keep=False,
            )

        def wait(self, dp, dq, c):
            arrived(self.part(dp, dq, c), self.rsem.at[dq * 4 + dp, c])

        def spread(self, dp, c):
            self.copy(dp, 0, 0, 1, c)
            self.copy(dp, 0, 0, -1, c)

        def start(self, c):
            self.copy(0, 0, 1, 0, c)
            self.copy(0, 0, -1, 0, c)
            self.spread(0, c)

        def first(self, c):
            self.wait(3, 0, c)
            self.copy(3, 0, 1, 0, c)
            self.spread(3, c)
            self.wait(1, 0, c)
            self.spread(1, c)
            self.wait(0, 1, c)
            self.copy(0, 1, 0, -1, c)

        def second(self, c):
            self.wait(2, 0, c)
            self.spread(2, c)
            self.wait(3, 3, c)
            self.copy(3, 3, 0, 1, c)
            self.wait(1, 1, c)
            self.copy(1, 1, 0, -1, c)

        def third(self, c):
            self.wait(2, 3, c)
            self.copy(2, 3, 0, 1, c)

        def last(self, *slots):
            for c in range(rows // self.size):
                for dp, dq in slots:
                    self.wait(dp, dq, c)

        def run(self, step):
            for c in range(rows // self.size):
                step(c)

    images = Plane(fb, b_send, b_recv, chunk)

    col = lax.broadcasted_iota(jnp.int32, (width, 128), 0)
    combo = (col * 911) >> 17
    rest = col - 144 * combo
    layer = (rest * 3641) >> 16
    source = 18 * (32 * (combo >> 2) + 4 * layer + (combo & 3)) + rest - 18 * layer
    lane = lax.broadcasted_iota(jnp.int32, (width, 128), 1)
    for j in range(width // 128):
        order[:, 128 * j : 128 * (j + 1)] = jnp.where(source == lane + 128 * j, 1.0, 0.0).astype(BF16)
    inputs[0].wait()
    text = text_ref[...].astype(F32)
    text_inv = lax.rsqrt(jnp.sum(text * text, axis=1, keepdims=True) + 1e-06)
    own_a = SLOT_ROW[("O", "0")] * rows
    own_b = PLANE_ROW[0, 0] * rows
    ta[own_a : own_a + rows] = (text * text_inv).astype(BF16)

    pl.semaphore_wait(barrier, len(peers))
    a_start()
    inputs[1].wait()
    fb[own_b : own_b + rows] = lax.dot_general(
        feats_ref[...], order[...], (((1,), (1,)), ((), ())), preferred_element_type=F32
    ).astype(BF16)
    images.run(images.start)
    zs[...] = jnp.zeros_like(zs)
    ext[...] = jnp.zeros_like(ext)
    loss_send[...] = jnp.zeros_like(loss_send)

    def weight(b):
        r = slice(384 * b, 384 * (b + 1))
        wp[r, :] = jnp.dot(order[r, :], wv[...], preferred_element_type=F32).astype(BF16)

    for copy in inputs[2:]:
        copy.wait()
    weight(0)
    a_step(1)
    weight(1)

    half = 8 * rows

    def project(lo, hi):
        r = slice(lo * rows, hi * rows)
        zproj = jnp.dot(fb[r, :], wp[...], preferred_element_type=F32)
        img_inv = lax.rsqrt(jnp.sum(zproj * zproj, axis=1, keepdims=True) + 1e-06)
        ub[r, :] = (zproj * img_inv).astype(BF16)
        inv[r, :] = jnp.broadcast_to(img_inv, ((hi - lo) * rows, 128))

    scale = jnp.exp(jnp.full((1, 128), scale_ref[0], F32))[:, :1]
    shift = shift_ref[0]
    def cell(batch, pair):
        r0, r1 = (rows * b for b in BATCHES[batch])
        prod = lax.dot_general(
            ta[r0:r1, :], ub[pair * half : (pair + 1) * half, :], (((1,), (1,)), ((), ())),
            preferred_element_type=F32,
        )
        for j in range(half // 128):
            lanes = slice(128 * j, 128 * (j + 1))
            logit = scale * prod[:, lanes] + shift
            factor = scale
            if j == 0 and pair == 1 and r1 > own_a:
                row = lax.broadcasted_iota(jnp.int32, logit.shape, 0) + (r0 - own_a)
                own = row == lax.broadcasted_iota(jnp.int32, logit.shape, 1)
                logit = jnp.where(own, -logit, logit)
                factor = jnp.where(own, -scale, scale)
            e = jnp.exp(logit)
            g[pair, r0:r1, lanes] = (factor * (e / (1.0 + e))).astype(BF16)
            total = jnp.sum(jnp.log1p(e).reshape((r1 - r0) // 8, 8, 128), axis=0)
            if batch == 2:
                loss_acc[pair, :, lanes] = total
            else:
                loss_acc[pair, :, lanes] += total

    def image_half(pair):
        r = slice(pair * half, (pair + 1) * half)
        d = lax.dot_general(g[pair], ta[...], (((0,), (0,)), ((), ())), preferred_element_type=F32)
        u = ub[r, :].astype(F32)
        dzb[r, :] = (inv[r, :1] * (d - u * jnp.sum(u * d, axis=1, keepdims=True))).astype(BF16)

    images.run(images.first)
    weight(2)
    a_step(2)
    images.last((0, 3))
    project(8, 13)
    images.run(images.second)
    a_step(3)
    project(13, 16)
    a_finish("0", "L1", "S1")
    cell(2, 1)
    images.run(images.third)
    a_finish("L2", "S2")
    cell(1, 1)
    a_step(4)
    images.last((3, 1), (1, 3), (0, 2))
    project(0, 3)
    a_finish("L3", "S3", "L4")
    cell(0, 1)
    image_half(1)
    images.last((2, 1), (3, 2), (1, 2), (2, 2))
    project(3, 8)
    cell(2, 0)
    cell(1, 0)
    cell(0, 0)
    image_half(0)

    block = 384
    for b in range(width // block):
        r = slice(b * block, (b + 1) * block)
        out = lax.dot_general(fb[:, r], dzb[...], (((0,), (0,)), ((), ())), preferred_element_type=F32)
        qf[r, :] = out
        qb[r, :] = out.astype(BF16)
        for yl in range(2):
            lanes = pl.ds(pl.multiple_of(256 * (1 - core) + 512 * yl, 128), 384)
            send(qb.at[r, lanes], pq.at[yl, r], pq_send, pq_recv, partner, keep=False)

    def slot_rows(slot, c=None):
        if c is None:
            return pl.ds(SLOT_ROW[slot] * rows, rows)
        return pl.ds(SLOT_ROW[slot] * rows + c * chunk, chunk)

    def text_batch(b):
        lo, hi = BATCHES[b]
        r = slice(lo * rows, hi * rows)
        acc = jnp.dot(g[0, r, :], ub[:half], preferred_element_type=F32)
        acc += jnp.dot(g[1, r, :], ub[half:], preferred_element_type=F32)
        d_text[r, :] = acc
        for kind, name in SLOTS[lo:hi]:
            if kind == "X":
                i = STREAM.index(name)
                psend[i] = d_text[slot_rows((kind, name)), :].astype(BF16)
                send(psend.at[i], precv.at[i], ps_sem, pr_sem.at[i], partner, keep=False)

    def handed(name):
        i = STREAM.index(name)
        arrived(precv.at[i], pr_sem.at[i])

    def gathered(name, c):
        r = slice(c * chunk, (c + 1) * chunk)
        value = d_text[slot_rows(("O", name), c), :] + precv[STREAM.index(name), r].astype(F32)
        if name == "0":
            before = ["L1", "S1"]
        elif name in ("L4", "S3"):
            before = []
        else:
            before = [name[0] + str(int(name[1]) + 1)]
        for prev in before:
            j = RING.index(prev)
            arrived(rrecv.at[j, r], rr_sem.at[j, c])
            value = value + rrecv[j, r].astype(F32)
        return value

    def ring(*names):
        for name in names:
            handed(name)
        for c in range(n_chunk):
            r = slice(c * chunk, (c + 1) * chunk)
            for name in names:
                i = RING.index(name)
                rsend[i, r] = gathered(name, c).astype(BF16)
                send(
                    rsend.at[i, r], rrecv.at[i, r], rs_sem, rr_sem.at[i, c],
                    against if name[0] == "L" else along, keep=False,
                )

    def unit(dp, dq):
        px = (x + dp * (1 - core) + dq * core) % NX
        py = (y + dp * core + dq * (1 - core)) % NY
        r = pl.ds(pl.multiple_of(144 * ((py // 2) * NX + px), 16), 144)
        lanes = pl.ds(pl.multiple_of(256 * core + 512 * (py % 2), 128), 384)
        return qf[r, lanes] + pq[py % 2, r, :].astype(F32)

    text_batch(0)
    arrived(pq, pq_recv)
    for dp in (2, 1, 3, 0):
        for dq in (2, 1, 3):
            qs[dq - 1, dp] = unit(dp, dq).astype(BF16)
            send(
                qs.at[dq - 1, dp], qr.at[dq - 1, dp], qs_sem, qr_sem.at[dq - 1, dp], dev_b(0, dq), keep=False,
            )
    for dp in range(4):
        qo[dp] = unit(dp, 0)
    for pair in range(2):
        summed = jnp.sum(loss_acc[pair], axis=0, keepdims=True)
        for k in range(8):
            loss_send[8 * pair + k, :1, :rows] = summed[:, k * rows : (k + 1) * rows]
    for k, (dp, dq) in enumerate(PLANE_SLOTS):
        if (dp, dq) != (0, 0):
            i = ((4 - dq) % 4) * 4 + (4 - dp) % 4
            send(loss_send.at[k], loss_recv.at[i], l_send, l_recv, dev_b(dp, dq), keep=False)

    text_batch(1)
    ring("L4")
    text_batch(2)
    ring("L3", "S3")

    def mine(dp):
        total = qo[dp]
        for i in (0, 2, 1):
            arrived(qr.at[i, dp], qr_sem.at[i, dp])
            total = total + qr[i, dp].astype(F32)
        return total

    def plane(dp):
        ps[dp - 1] = mine(dp).astype(BF16)
        send(ps.at[dp - 1], pr.at[dp - 1], ts_sem, tr_sem, dev_b(dp, 0), keep=False)

    plane(2)
    ring("L2", "S2")
    plane(1)
    plane(3)
    ring("L1", "S1")
    own = mine(0)
    arrived(pr, tr_sem)
    for i in (0, 2, 1):
        own = own + pr[i].astype(F32)
    fz[...] = own
    for tz in range(NZ):
        piece = fz[18 * tz : 18 * tz + 18, :]
        zf[tz, :18] = piece
        zs[tz, :, :384] = piece[:16].astype(BF16)
        for t in range(3):
            ext[2 * t : 2 * t + 2, :] = fz[18 * tz + 16 : 18 * tz + 18, 128 * t : 128 * (t + 1)]
        zs[tz, :, 384:] = ext[...].astype(BF16)
    for dz in (4, 3, 5, 2, 6, 1, 7):
        send(zs.at[(z + dz) % NZ], zr.at[NZ - dz], zs_sem, zr_sem, dev(dz=dz), keep=False)

    handed("0")
    for c in range(n_chunk):
        dtext_out[c * chunk : (c + 1) * chunk] = gathered("0", c)
    loss = loss_send[PLANE_ROW[0, 0]]
    arrived(loss_recv.at[pl.ds(1, 15)], l_recv)
    for i in range(1, 16):
        loss = loss + loss_recv[i]
    loss_out[...] = loss
    outputs = [
        pltpu.make_async_copy(src, dst, out_sem.at[i])
        for i, (src, dst) in enumerate(((loss_out, loss_hbm), (dtext_out, dtext_hbm), (dproj_out, dproj_hbm)))
    ]
    outputs[0].start()
    outputs[1].start()
    acc = jnp.zeros((16, 512), F32)
    arrived(zr.at[pl.ds(1, 7)], zr_sem)
    for dz in range(1, 8):
        acc = acc + zr[dz].astype(F32)
    fin[:16] = zf[z, :16] + acc[:, :384]
    for t in range(3):
        fin[16:18, 128 * t : 128 * (t + 1)] = zf[z, 16:18, 128 * t : 128 * (t + 1)] + acc[2 * t : 2 * t + 2, 384:]
    for n in range(4):
        @pl.when(narrow == n)
        def _():
            dproj_out[...] = fin[:18, 32 * n : 32 * n + 288]

    outputs[2].start()
    for copy in sends:
        copy.wait_send()
    for buf, ssem in ((rsend, rs_sem), (psend, ps_sem), (qs, qs_sem), (ps, ts_sem), (pq, pq_send)):
        sent(buf, ssem)
    sent(zs.at[pl.ds(0, 7)], zs_sem)
    sent(ta.at[pl.ds(0, 15 * rows)], a_send)
    sent(fb.at[pl.ds(0, 15 * rows)], b_send)
    sent(loss_send.at[pl.ds(0, 15)], l_send)
    for copy in outputs:
        copy.wait()


def results(loss_ref, dtext_ref, dproj_ref, loss_out, dtext_out, dproj_out):
    loss_out[...] = loss_ref[:1, : loss_out.shape[1]]
    dtext_out[...] = dtext_ref[...]
    dproj_out[...] = dproj_ref[...]


def local(image_feats, proj_weight, text_embed, log_scale, logit_bias):
    rows, width = image_feats.shape
    vmem = pl.BlockSpec(memory_space=pltpu.VMEM)
    anywhere = pl.BlockSpec(memory_space=pl.ANY)
    group = 16 * rows
    dma = pltpu.SemaphoreType.DMA
    loss, d_text, d_proj = pl.pallas_call(
        kernel,
        out_shape=(
            jax.ShapeDtypeStruct((8, 128), F32),
            jax.ShapeDtypeStruct((rows, width), F32),
            jax.ShapeDtypeStruct((width // 64, width // 4), F32),
        ),
        in_specs=[pl.BlockSpec(memory_space=pltpu.HBM)] * 5,
        out_specs=(anywhere, anywhere, anywhere),
        scratch_shapes=[
            pltpu.SMEM((1,), F32),
            pltpu.SMEM((1,), F32),
            pltpu.VMEM((rows, width), BF16),
            pltpu.VMEM((rows, width), BF16),
            pltpu.VMEM((width, width), BF16),
            pltpu.VMEM((width, width), BF16),
            pltpu.VMEM((width, width), BF16),
            pltpu.VMEM((group, width), BF16),
            pltpu.VMEM((group, width), BF16),
            pltpu.VMEM((group, width), BF16),
            pltpu.VMEM((group, 128), F32),
            pltpu.VMEM((2, group, group // 2), BF16),
            pltpu.VMEM((2, 8, group // 2), F32),
            pltpu.VMEM((16, 8, 128), F32),
            pltpu.VMEM((16, 8, 128), F32),
            pltpu.VMEM((group, width), F32),
            pltpu.VMEM((8, rows, width), BF16),
            pltpu.VMEM((8, rows, width), BF16),
            pltpu.VMEM((7, rows, width), BF16),
            pltpu.VMEM((7, rows, width), BF16),
            pltpu.VMEM((group, width), BF16),
            pltpu.VMEM((width, width), F32),
            pltpu.VMEM((width, width), BF16),
            pltpu.VMEM((2, width, 384), BF16),
            pltpu.VMEM((3, 4, 144, 384), BF16),
            pltpu.VMEM((4, 144, 384), F32),
            pltpu.VMEM((3, 4, 144, 384), BF16),
            pltpu.VMEM((3, 144, 384), BF16),
            pltpu.VMEM((3, 144, 384), BF16),
            pltpu.VMEM((144, 384), F32),
            pltpu.VMEM((8, 24, 384), F32),
            pltpu.VMEM((8, 16, 512), BF16),
            pltpu.VMEM((8, 16, 512), BF16),
            pltpu.VMEM((16, 128), F32),
            pltpu.VMEM((24, 384), F32),
            pltpu.VMEM((8, 128), F32),
            pltpu.VMEM((rows, width), F32),
            pltpu.VMEM((width // 64, width // 4), F32),
            dma((5,)), dma((3,)), dma, dma((8, 3)), dma((8,)),
            dma, dma((16, 3)),
            dma, dma, dma, dma((8,)), dma, dma((7, 3)),
            dma, dma,
            dma, dma((3, 4)), dma, dma, dma, dma,
        ],
        compiler_params=pltpu.CompilerParams(
            collective_id=0, has_side_effects=True, vmem_limit_bytes=60 * 1024 * 1024
        ),
    )(log_scale, logit_bias, image_feats, proj_weight, text_embed)
    loss, d_text, d_proj = pl.pallas_call(
        results,
        out_shape=(
            jax.ShapeDtypeStruct((1, rows), F32),
            jax.ShapeDtypeStruct(d_text.shape, F32),
            jax.ShapeDtypeStruct(d_proj.shape, F32),
        ),
        in_specs=[vmem, vmem, vmem],
        out_specs=(vmem, vmem, vmem),
    )(loss, d_text, d_proj)
    return loss.reshape(rows), d_text, d_proj


def solution(mesh):
    placed = (P(("wide", "narrow"), None), P(), P(("wide", "narrow"), None), P(), P())
    return jax.shard_map(
        local,
        mesh=mesh,
        in_specs=placed,
        out_specs=(P(("wide", "narrow")), P(("wide", "narrow"), None), P("wide", "narrow")),
        check_vma=False,
    )
```
